32 devices in a mesh: groups: 2 (over y), blk: 4 (over x, core), ulysses: 4 (over z).
Axes of the slice: x: 2, y: 2, z: 4, core: 2. Of those that a mesh axis runs over, the one named last changes fastest.
Arguments:
- query_proj: bfloat16 [1024, 1024], P(('groups', 'blk', 'ulysses')), parts along dimension 0, may hold values from -200 to 200
- key_proj: bfloat16 [1024, 1024], P(('groups', 'blk', 'ulysses')), parts along dimension 0, may hold values from -200 to 200
- value_proj: bfloat16 [1024, 1024], P(('groups', 'blk', 'ulysses')), parts along dimension 0, may hold values from -6 to 6
- query_gain: float32 [1024], replicated, may hold values from 1.2 to 2.4
- key_gain: float32 [1024], replicated, may hold values from 1.2 to 2.4
- control: bfloat16 [1024, 384], P(('groups', 'blk', 'ulysses')), parts along dimension 0, may hold values from -6 to 6
- hint_weight: bfloat16 [384, 1024], replicated, may hold values from -0.3125 to 0.3125
- hint_gain: float32 [8, 1024], replicated, may hold values from 0.3 to 3
- owner_map: int32 [32, 4], P(('groups', 'blk', 'ulysses')), parts along dimension 0, may hold values from 0 to 3, each once within a row
- layer_index: int32 [32], P(('groups', 'blk', 'ulysses')), parts along dimension 0, may hold values from 0 to 7
Outputs:
- block_out: bfloat16 [1024, 1024], P(('groups', 'blk', 'ulysses')), parts along dimension 0
The draws below stay inside these ranges and needn't reach their ends.
There are 2 independent parts, one for each index of `groups`. The reference program is written for one: setup_inputs(seed, part) draws one part's arguments, and reference() takes and returns one part's arrays. A program takes and returns all parts, laid end to end along the dimension named above; an argument that names none is the same for every part. Nothing has to cross between parts.
Inputs may be any that keep to these rules, and one draw needn't show every extreme that they name: `owner_map`: each row is a permutation of 0 to 3.
All inputs are finite; a program needn't handle non-finite values.
Results may differ from the reference program's by a relative error of at most 0.008.
Values may be sent and summed in bfloat16 or wider, within the bound.
A program may use at most 64 MiB of HBM per device.

```python
import math
import jax
import jax.numpy as jnp
from jax import lax

HEAD_DIM = 128
HEADS = 8
FEATS = 1024
CTRL_IN = 384
CTRL_LAYERS = 8
TOK_DEV = 32
SLAB = 8
TOKENS = 512
N_BLK = 4
N_ULYSSES = 4


def paired_draw(key):
    base_q = jax.random.fold_in(key, 11)
    base_k = jax.random.fold_in(key, 12)
    column_key = jax.random.fold_in(key, 13)
    columns = jnp.exp(jax.random.uniform(column_key, (FEATS,), jnp.float32, 0.0, 2.302585))
    query_rows = jax.random.truncated_normal(base_q, -4.0, 4.0, (TOKENS, FEATS), jnp.float32) * columns
    key_rows = jax.random.truncated_normal(base_k, -4.0, 4.0, (TOKENS, FEATS), jnp.float32) * columns
    query_rows = jnp.clip(query_rows, -200.0, 200.0)
    key_rows = jnp.clip(key_rows, -200.0, 200.0)
    return (query_rows, key_rows)


def draw_query_proj(key, part):
    return paired_draw(key)[0].astype(jnp.bfloat16)


def draw_key_proj(key, part):
    return paired_draw(key)[1].astype(jnp.bfloat16)


def set_ends(entries, key, smallest, high):
    shape = entries.shape
    place = [jax.random.randint(jax.random.fold_in(key, axis), (), 0, shape[axis]) for axis in range(len(shape))]
    entries = entries.at[tuple(place)].set(smallest)
    longest = shape.index(max(shape))
    place[longest] = (place[longest] + 1) % shape[longest]
    return entries.at[tuple(place)].set(high)


def block_levels(key, extent, cuts, low, top_value):
    level = 1.0
    for axis_at, blocks in cuts:
        steps = jax.random.uniform(jax.random.fold_in(jax.random.fold_in(key, 6), axis_at), (blocks,), jnp.float32, low / len(cuts), top_value / len(cuts))
        level = level * jnp.repeat(jnp.exp(steps), extent[axis_at] // blocks).reshape((-1,) + (1,) * (len(extent) - 1 - axis_at))
    return level


def normal_values(own_key, dims, deviation, most, shards=(), held_as=jnp.bfloat16):
    level = block_levels(own_key, dims, shards, -0.22, 0.18) if shards else 1.0
    values = jax.random.normal(own_key, dims, jnp.float32) * deviation * level
    return jnp.minimum(jnp.maximum(values, -most), most).astype(held_as)


def setup_inputs(seed: int = 0, part: int = 0) -> dict:
    key_list = jax.random.split(jax.random.key(seed), 11)
    own_keys = jax.random.split(jax.random.fold_in(key_list[10], part), 11)
    query_proj = draw_query_proj(jax.random.fold_in(jax.random.fold_in(key_list[10], part), 71), part)
    key_proj = draw_key_proj(jax.random.fold_in(jax.random.fold_in(key_list[10], part), 71), part)
    value_proj = normal_values(own_keys[2], (TOKENS, FEATS), 1.0, 6.0, ((0, 16),))
    query_gain = jnp.clip(jax.random.uniform(key_list[3], (FEATS,), jnp.float32, 1.2, 2.4), 1.2, 2.4)
    key_gain = jnp.clip(jax.random.uniform(key_list[4], (FEATS,), jnp.float32, 1.2, 2.4), 1.2, 2.4)
    control = normal_values(own_keys[5], (TOKENS, CTRL_IN), 1.0, 6.0, ((0, 16),))
    hint_weight = normal_values(key_list[6], (CTRL_IN, FEATS), CTRL_IN ** -0.5, 0.3125)
    hint_gain = jnp.clip(jnp.exp(jax.random.uniform(key_list[7], (CTRL_LAYERS, FEATS), jnp.float32, math.log(0.3), math.log(3.0))), 0.3, 3.0)
    owner_map = jax.vmap(lambda own: jax.random.permutation(own, N_ULYSSES))(jax.random.split(own_keys[8], (N_BLK * N_ULYSSES))).reshape((N_BLK * N_ULYSSES, N_ULYSSES)).astype(jnp.int32)
    layer_index = set_ends(jax.random.randint(own_keys[9], (N_BLK * N_ULYSSES,), 0, CTRL_LAYERS), jax.random.fold_in(own_keys[9], 1), 0, CTRL_LAYERS - 1).astype(jnp.int32)
    return dict(query_proj=query_proj, key_proj=key_proj, value_proj=value_proj, query_gain=query_gain, key_gain=key_gain, control=control, hint_weight=hint_weight, hint_gain=hint_gain, owner_map=owner_map, layer_index=layer_index)


def normalize_rows(rows, gain):
    values = rows.astype(jnp.float32)
    scale = lax.rsqrt(lax.optimization_barrier(jnp.mean(values * values, axis=-1, keepdims=True)) + 1e-06)
    return (values * scale * gain).astype(jnp.bfloat16)

def query_block_size(count):
    block = min(count, 1024)
    while count % block:
        block = block - 1
    return block

def one_head(triple):
    queries, keys, values = triple
    count = queries.shape[0]
    block = query_block_size(count)
    shaped = queries.reshape(count // block, block, HEAD_DIM)

    def per_block(query_rows):
        scores = jnp.dot(query_rows, keys.T, preferred_element_type=jnp.float32) * HEAD_DIM ** (-0.5)
        peak = lax.optimization_barrier(jnp.max(scores, axis=-1, keepdims=True))
        expo = jnp.exp(scores - peak)
        totals = lax.optimization_barrier(jnp.sum(expo, axis=-1, keepdims=True))
        probs = expo.astype(jnp.bfloat16)
        mixed = jnp.dot(probs, values, preferred_element_type=jnp.float32)
        return (mixed / totals).astype(jnp.bfloat16)
    return lax.map(per_block, shaped).reshape(count, HEAD_DIM)

def reference(query_proj, key_proj, value_proj, query_gain, key_gain, control, hint_weight, hint_gain, owner_map, layer_index):
    count = query_proj.shape[0]
    query_normed = normalize_rows(query_proj, query_gain)
    key_normed = normalize_rows(key_proj, key_gain)
    split_q = query_normed.reshape(count, HEADS, HEAD_DIM).transpose(1, 0, 2)
    split_k = key_normed.reshape(count, HEADS, HEAD_DIM).transpose(1, 0, 2)
    split_v = value_proj.reshape(count, HEADS, HEAD_DIM).transpose(1, 0, 2)
    attended = lax.map(one_head, (split_q, split_k, split_v))
    attended = attended.transpose(1, 0, 2).reshape(count, FEATS)
    control_normed = normalize_rows(control, jnp.float32(1.0))
    hint = jnp.dot(control_normed, hint_weight, preferred_element_type=jnp.float32).astype(jnp.bfloat16)
    slabs = hint.reshape(N_BLK, N_ULYSSES, N_ULYSSES, SLAB, FEATS)
    owners = owner_map.reshape(N_BLK, N_ULYSSES, N_ULYSSES)
    positions = jnp.arange(N_ULYSSES, dtype=jnp.int32)
    match = (owners[:, :, :, None] == positions[None, None, None, :]).astype(jnp.int32)
    inverse = lax.optimization_barrier(jnp.sum(positions[None, None, :, None] * match, axis=2)).astype(jnp.int32)
    picked = jnp.take_along_axis(slabs, inverse[:, :, :, None, None], axis=2)
    placed = picked.transpose(0, 2, 1, 3, 4).reshape(N_BLK * N_ULYSSES, TOK_DEV, FEATS)
    gains = jnp.take(hint_gain, layer_index.astype(jnp.int32), axis=0)
    scaled = (placed.astype(jnp.float32) * gains[:, None, :]).reshape(count, FEATS)
    return (attended.astype(jnp.float32) + scaled).astype(jnp.bfloat16)
```

```python
import functools
import math

import jax
import jax.numpy as jnp
from jax import lax
from jax.experimental import pallas as pl
from jax.experimental.pallas import tpu as pltpu
from jax.sharding import PartitionSpec as P

HEAD_DIM = 128
CORES = 2
MESH = pl.DeviceIdType.MESH


def normalize_rows(rows, gain):
    values = rows.astype(jnp.float32)
    scale = lax.rsqrt(jnp.mean(values * values, axis=-1, keepdims=True) + 1e-06)
    return (values * scale * gain).astype(jnp.bfloat16)


def block_size(count):
    block = min(count, 1024)
    while count % block:
        block = block - 1
    return block


def make_fold(queries):
    rows = queries.shape[0]
    heads = queries.shape[1] // HEAD_DIM
    shaped = queries.reshape(rows, heads, HEAD_DIM)
    factor = HEAD_DIM ** (-0.5)

    def update(state, pair):
        peak, totals, accum = state
        key_block, value_block = pair
        scores = (
            jnp.einsum("qhd,khd->hqk", shaped, key_block, preferred_element_type=jnp.float32)
            * factor
        )
        new_peak = jnp.maximum(peak, jnp.max(scores, axis=-1))
        correction = jnp.exp(peak - new_peak)
        expo = jnp.exp(scores - new_peak[:, :, None])
        totals = totals * correction + jnp.sum(expo, axis=-1)
        mixed = jnp.einsum(
            "hqk,khd->hqd",
            expo.astype(jnp.bfloat16),
            value_block,
            preferred_element_type=jnp.float32,
        )
        accum = accum * correction[:, :, None] + mixed
        return ((new_peak, totals, accum), None)

    def fold(carry, piece, start):
        keys, values = piece
        count = keys.shape[0]
        block = block_size(count)
        key_blocks = keys.reshape(count // block, block, heads, HEAD_DIM)
        value_blocks = values.reshape(count // block, block, heads, HEAD_DIM)
        result, unused = lax.scan(update, carry, (key_blocks, value_blocks))
        return result

    start_state = (
        jnp.full((heads, rows), -1e30, jnp.float32),
        jnp.zeros((heads, rows), jnp.float32),
        jnp.zeros((heads, rows, HEAD_DIM), jnp.float32),
    )
    return (fold, start_state)


def finish(state):
    peak, totals, accum = state
    heads, rows = totals.shape
    output = (accum / totals[:, :, None]).astype(jnp.bfloat16)
    return output.transpose(1, 0, 2).reshape(rows, heads * HEAD_DIM)


def make_hint(patches, hint_weight):
    normed = normalize_rows(patches, jnp.float32(1.0))
    return jnp.dot(normed, hint_weight, preferred_element_type=jnp.float32).astype(jnp.bfloat16)


def shards(
    query_proj,
    key_proj,
    value_proj,
    query_gain,
    key_gain,
    control,
    hint_weight,
    hint_gain,
    owner_map,
    layer_index,
):
    query_normed = normalize_rows(query_proj, query_gain)
    key_normed = normalize_rows(key_proj, key_gain)
    query_heads, key_heads, value_heads = (
        lax.all_to_all(query_normed, "ulysses", split_axis=1, concat_axis=0, tiled=True),
        lax.all_to_all(key_normed, "ulysses", split_axis=1, concat_axis=0, tiled=True),
        lax.all_to_all(value_proj, "ulysses", split_axis=1, concat_axis=0, tiled=True),
    )
    fold, start_state = make_fold(query_heads)
    state = fold(
        start_state,
        (
            lax.all_gather(key_heads, "blk", axis=0, tiled=True),
            lax.all_gather(value_heads, "blk", axis=0, tiled=True),
        ),
        jnp.int32(0),
    )
    attended = lax.all_to_all(finish(state), "ulysses", split_axis=0, concat_axis=1, tiled=True)
    owners = lax.axis_size("ulysses")
    tok_rows = control.shape[0]
    slab_rows = tok_rows // owners
    positions = jnp.arange(owners, dtype=jnp.int32)
    match = (owner_map[0][:, None] == positions[None, :]).astype(jnp.int32)
    inverse = jnp.sum(positions[:, None] * match, axis=0)
    gain_row = lax.dynamic_index_in_dim(hint_gain, layer_index[0], 0, keepdims=False)
    outgoing = jnp.take(control.reshape(owners, slab_rows, control.shape[1]), inverse, axis=0)
    arrived = lax.all_to_all(outgoing, "ulysses", split_axis=0, concat_axis=0, tiled=True).reshape(
        tok_rows, control.shape[1]
    )
    placed = make_hint(arrived, hint_weight)
    return (attended.astype(jnp.float32) + placed.astype(jnp.float32) * gain_row).astype(
        jnp.bfloat16
    )


def row_scale(values):
    return lax.rsqrt(jnp.mean(values * values, axis=-1, keepdims=True) + 1e-06)


def kernel(
    blks,
    owners,
    query_hbm,
    key_hbm,
    value_hbm,
    query_gain_hbm,
    key_gain_hbm,
    control_hbm,
    weight_hbm,
    gain_hbm,
    owner_hbm,
    layer_smem,
    out_ref,
    query_in,
    key_in,
    query_gain,
    key_gain,
    control_in,
    weight,
    gains,
    owner_smem,
    stage,
    landed,
    slabs_out,
    slabs_in,
    mixed_out,
    attended,
    hint,
    load_sem,
    value_sem,
    send_sem,
    recv_sem,
    slab_send,
    slab_recv,
    back_send,
    back_recv,
    far_sem,
    line_sem,
):
    rows = query_in.shape[0]
    low, high = host_range(owners)
    wide = high - low
    heads = blks * wide
    cols = blks // CORES
    devices = blks * owners
    slab_rows = rows // owners
    b = lax.axis_index("blk")
    u = lax.axis_index("ulysses")
    x = b // CORES
    me = b * owners + u
    own = b * wide + u - low
    hosting = (u >= low) & (u < high)
    visiting = jnp.logical_not(hosting)
    near_low = 2 * u < owners
    near = jnp.where(near_low, low, high - 1)
    far = jnp.where(near_low, high - 1, low)
    edge = jnp.where(near_low, 0, owners - 1)
    partner = {"blk": x * CORES + (1 - lax.rem(b, CORES))}

    def signal(semaphore, device):
        pl.semaphore_signal(semaphore, inc=1, device_id=device, device_id_type=MESH)

    barrier = pltpu.get_barrier_semaphore()
    for to_b in range(blks):
        signal(barrier, {"blk": to_b, "ulysses": jnp.where(hosting, far, near)})

    @pl.when(hosting)
    def _():
        for to_b in range(blks):
            signal(barrier, {"blk": to_b, "ulysses": edge})

            @pl.when(to_b != b)
            def _():
                signal(barrier, {"blk": to_b})

    loads = [
        pltpu.make_async_copy(source, target, load_sem.at[at])
        for at, (source, target) in enumerate(
            (
                (query_hbm, query_in),
                (query_gain_hbm, query_gain),
                (key_hbm, key_in),
                (key_gain_hbm, key_gain),
                (control_hbm, control_in),
                (owner_hbm, owner_smem),
                (weight_hbm, weight),
                (gain_hbm, gains),
            )
        )
    ]
    for load in loads:
        load.start()

    def remote(source, target, sem_out, sem_in, device):
        return pltpu.make_async_remote_copy(
            src_ref=source,
            dst_ref=target,
            send_sem=sem_out,
            recv_sem=sem_in,
            device_id=device,
            device_id_type=MESH,
        )

    def drain(target, semaphore):
        pltpu.make_async_copy(target, target, semaphore).wait()

    values_at, normed_at = pl.ds(2 * rows, rows), pl.ds(0, 2 * rows)

    def columns_of(h):
        return pl.ds(pl.multiple_of(h * HEAD_DIM, HEAD_DIM), HEAD_DIM)

    def send(source, span, core, to_u):
        for aside in (*range(1, cols), 0):
            to_b = lax.rem(x + aside, cols) * CORES + core

            @pl.when((to_b != b) | (to_u != u))
            def _():
                h = to_b * wide + to_u - low
                remote(
                    source(h),
                    landed.at[me, span],
                    send_sem,
                    recv_sem,
                    {"blk": to_b, "ulysses": to_u},
                ).start()

    def send_values(to_u):
        for core in range(CORES):
            send(lambda h: value_hbm.at[:, columns_of(h)], values_at, core, to_u)

    own_values = pltpu.make_async_copy(
        value_hbm.at[:, columns_of(jnp.where(hosting, own, 0))],
        landed.at[me, values_at],
        value_sem,
    )

    @pl.when(hosting)
    def _():
        own_values.start()
        pl.semaphore_wait(barrier, 3 * blks - 1)
        signal(far_sem, {"ulysses": edge})
        signal(far_sem, {"ulysses": far})
        send_values(far)
        send_values(near)

    @pl.when(visiting)
    def _():
        pl.semaphore_wait(barrier, blks)
        send_values(near)

    for load in loads[:4]:
        load.wait()
    for first, gain, part in ((query_in, query_gain, 0), (key_in, key_gain, 1)):
        values = first[...].astype(jnp.float32)
        normed = (values * row_scale(values) * gain[...]).astype(jnp.bfloat16)
        for h in range(heads):
            stage[h, part * rows : (part + 1) * rows] = normed[
                :, h * HEAD_DIM : (h + 1) * HEAD_DIM
            ]

    @pl.when(visiting)
    def _():
        pl.semaphore_wait(far_sem, 1)
        send_values(far)

    for core in range(CORES):
        for to_u in (far, near):
            send(lambda h: stage.at[h], normed_at, core, to_u)

    loads[4].wait()
    loads[5].wait()
    values = control_in[...].astype(jnp.float32)
    normed = values * row_scale(values)
    pieces = [normed[j * slab_rows : (j + 1) * slab_rows] for j in range(owners)]
    for to in range(owners):
        picked = pieces[0]
        for j in range(1, owners):
            picked = jnp.where(owner_smem[0, j] == to, pieces[j], picked)
        slabs_out[to] = picked.astype(jnp.bfloat16)

    @pl.when(hosting)
    def _():
        pl.semaphore_wait(far_sem, 1)
        signal(line_sem, {"ulysses": edge})

    @pl.when(visiting)
    def _():
        pl.semaphore_wait(line_sem, 1)

    for d in range(1, owners):
        there = lax.rem(u + d, owners)
        remote(
            slabs_out.at[there], slabs_in.at[u], slab_send, slab_recv, {"ulysses": there}
        ).start()
    slabs_in[u] = slabs_out[u]

    order = [
        (to_b, to_u)
        for to_u in sorted(range(owners), key=lambda at: (low <= at < high, at))
        for to_b in range(blks)
    ]
    factor = HEAD_DIM ** (-0.5) * math.log2(math.e)

    @pl.when(hosting)
    def _():
        landed[me, normed_at] = stage[own]
        own_values.wait()
        drain(landed.at[pl.ds(0, devices - 1)], recv_sem)

        count = devices * rows
        keys = landed[:, rows : 2 * rows].reshape(count, HEAD_DIM)
        mix = landed[:, 2 * rows :].reshape(count, HEAD_DIM)
        group = devices // GROUPS

        def flush(base):
            for to_b, to_u in order[base : base + group]:
                there = to_b * owners + to_u

                @pl.when(there != me)
                def _():
                    remote(
                        mixed_out.at[there],
                        attended.at[own],
                        back_send,
                        back_recv,
                        {"blk": to_b, "ulysses": to_u},
                    ).start()

        for base in range(0, devices, group):
            part = [to_b * owners + to_u for to_b, to_u in order[base : base + group]]
            queries = jnp.concatenate([landed[there, :rows] for there in part], axis=0)
            scores = lax.dot_general(
                queries, keys, (((1,), (1,)), ((), ())), preferred_element_type=jnp.float32
            )
            peak = jnp.max(scores, axis=-1, keepdims=True)
            expo = jnp.exp2((scores - peak) * factor)
            totals = jnp.sum(expo, axis=-1, keepdims=True)
            output = jnp.dot(
                expo.astype(jnp.bfloat16), mix, preferred_element_type=jnp.float32
            )
            output = (output * (1.0 / totals)).astype(jnp.bfloat16)
            for at, there in enumerate(part):
                mixed_out[there] = output[at * rows : (at + 1) * rows]
            flush(base)
        attended[own] = mixed_out[me]

    loads[6].wait()
    loads[7].wait()
    drain(slabs_in.at[pl.ds(0, owners - 1)], slab_recv)
    arrived = slabs_in[...].astype(jnp.float32).reshape(rows, control_in.shape[1])
    placed = jnp.dot(
        arrived.astype(jnp.bfloat16), weight[...], preferred_element_type=jnp.float32
    ).astype(jnp.bfloat16)
    hint[...] = placed.astype(jnp.float32) * gains[pl.ds(layer_smem[0], 1), :]
    drain(slabs_in.at[pl.ds(0, owners - 1)], slab_send)

    @pl.when(hosting)
    def _():
        drain(landed.at[pl.ds(0, heads - 1)], send_sem)
        drain(mixed_out.at[pl.ds(0, devices - 1)], back_send)
        drain(attended.at[pl.ds(0, heads - 1)], back_recv)

    @pl.when(visiting)
    def _():
        drain(landed.at[pl.ds(0, heads)], send_sem)
        drain(attended, back_recv)

    for h in range(heads):
        columns = slice(h * HEAD_DIM, (h + 1) * HEAD_DIM)
        out_ref[:, columns] = (attended[h].astype(jnp.float32) + hint[:, columns]).astype(
            jnp.bfloat16
        )


GROUPS = 4


def host_range(owners):
    low = owners // 4
    return (low, owners - low)


def run(blks, owners, *arrays):
    query_proj, control, hint_weight, hint_gain = arrays[0], arrays[5], arrays[6], arrays[7]
    rows, feats = query_proj.shape
    low, high = host_range(owners)
    heads = blks * (high - low)
    devices = blks * owners
    fits = (
        blks % CORES == 0
        and owners > 1
        and heads * HEAD_DIM == feats
        and (low, high) == (1, owners - 1)
        and high - low == 2
        and devices % GROUPS == 0
        and rows % 16 == 0
        and rows % owners == 0
        and (rows // owners) % 8 == 0
        and rows * devices <= 1024
    )
    if not fits:
        return shards(*arrays)
    inner = control.shape[1]
    dma = pltpu.SemaphoreType.DMA
    half = jnp.bfloat16
    wide = jnp.float32
    operands = list(arrays)
    operands[3] = arrays[3].reshape(1, feats)
    operands[4] = arrays[4].reshape(1, feats)
    layer = operands.pop()
    operands = [pltpu.with_memory_space_constraint(array, pltpu.HBM) for array in operands]
    return pl.pallas_call(
        functools.partial(kernel, blks, owners),
        out_shape=jax.ShapeDtypeStruct((rows, feats), half),
        in_specs=[pl.BlockSpec(memory_space=pltpu.HBM)] * len(operands)
        + [pl.BlockSpec(memory_space=pltpu.SMEM)],
        out_specs=pl.BlockSpec(memory_space=pltpu.VMEM),
        scratch_shapes=[
            pltpu.VMEM((rows, feats), half),
            pltpu.VMEM((rows, feats), half),
            pltpu.VMEM((1, feats), wide),
            pltpu.VMEM((1, feats), wide),
            pltpu.VMEM((rows, inner), half),
            pltpu.VMEM(hint_weight.shape, half),
            pltpu.VMEM(hint_gain.shape, wide),
            pltpu.SMEM((1, owners), jnp.int32),
            pltpu.VMEM((heads, 2 * rows, HEAD_DIM), half),
            pltpu.VMEM((devices, 3 * rows, HEAD_DIM), half),
            pltpu.VMEM((owners, rows // owners, inner), half),
            pltpu.VMEM((owners, rows // owners, inner), half),
            pltpu.VMEM((devices, rows, HEAD_DIM), half),
            pltpu.VMEM((heads, rows, HEAD_DIM), half),
            pltpu.VMEM((rows, feats), wide),
            dma((len(operands),)),
            dma,
            dma,
            dma,
            dma,
            dma,
            dma,
            dma,
            pltpu.SemaphoreType.REGULAR,
            pltpu.SemaphoreType.REGULAR,
        ],
        compiler_params=pltpu.CompilerParams(
            collective_id=0, has_side_effects=True, vmem_limit_bytes=16 << 20
        ),
    )(*operands, layer)


def solution(mesh):
    return jax.shard_map(
        functools.partial(run, mesh.shape["blk"], mesh.shape["ulysses"]),
        mesh=mesh,
        in_specs=(
            P(("groups", "blk", "ulysses"), None),
            P(("groups", "blk", "ulysses"), None),
            P(("groups", "blk", "ulysses"), None),
            P(),
            P(),
            P(("groups", "blk", "ulysses"), None),
            P(),
            P(),
            P(("groups", "blk", "ulysses"), None),
            P(("groups", "blk", "ulysses")),
        ),
        out_specs=P(("groups", "blk", "ulysses"), None),
        check_vma=False,
    )
```

```python
import functools
import math

import jax
import jax.numpy as jnp
from jax import lax
from jax.experimental import pallas as pl
from jax.experimental.pallas import tpu as pltpu
from jax.sharding import PartitionSpec as P

HEAD_DIM = 128
CORES = 2
MESH = pl.DeviceIdType.MESH


def normalize_rows(rows, gain):
    values = rows.astype(jnp.float32)
    scale = lax.rsqrt(jnp.mean(values * values, axis=-1, keepdims=True) + 1e-06)
    return (values * scale * gain).astype(jnp.bfloat16)


def block_size(count):
    block = min(count, 1024)
    while count % block:
        block = block - 1
    return block


def make_fold(queries):
    rows = queries.shape[0]
    heads = queries.shape[1] // HEAD_DIM
    shaped = queries.reshape(rows, heads, HEAD_DIM)
    factor = HEAD_DIM ** (-0.5)

    def update(state, pair):
        peak, totals, accum = state
        key_block, value_block = pair
        scores = (
            jnp.einsum("qhd,khd->hqk", shaped, key_block, preferred_element_type=jnp.float32)
            * factor
        )
        new_peak = jnp.maximum(peak, jnp.max(scores, axis=-1))
        correction = jnp.exp(peak - new_peak)
        expo = jnp.exp(scores - new_peak[:, :, None])
        totals = totals * correction + jnp.sum(expo, axis=-1)
        mixed = jnp.einsum(
            "hqk,khd->hqd",
            expo.astype(jnp.bfloat16),
            value_block,
            preferred_element_type=jnp.float32,
        )
        accum = accum * correction[:, :, None] + mixed
        return ((new_peak, totals, accum), None)

    def fold(carry, piece, start):
        keys, values = piece
        count = keys.shape[0]
        block = block_size(count)
        key_blocks = keys.reshape(count // block, block, heads, HEAD_DIM)
        value_blocks = values.reshape(count // block, block, heads, HEAD_DIM)
        result, unused = lax.scan(update, carry, (key_blocks, value_blocks))
        return result

    start_state = (
        jnp.full((heads, rows), -1e30, jnp.float32),
        jnp.zeros((heads, rows), jnp.float32),
        jnp.zeros((heads, rows, HEAD_DIM), jnp.float32),
    )
    return (fold, start_state)


def finish(state):
    peak, totals, accum = state
    heads, rows = totals.shape
    output = (accum / totals[:, :, None]).astype(jnp.bfloat16)
    return output.transpose(1, 0, 2).reshape(rows, heads * HEAD_DIM)


def make_hint(patches, hint_weight):
    normed = normalize_rows(patches, jnp.float32(1.0))
    return jnp.dot(normed, hint_weight, preferred_element_type=jnp.float32).astype(jnp.bfloat16)


def shards(
    query_proj,
    key_proj,
    value_proj,
    query_gain,
    key_gain,
    control,
    hint_weight,
    hint_gain,
    owner_map,
    layer_index,
):
    query_normed = normalize_rows(query_proj, query_gain)
    key_normed = normalize_rows(key_proj, key_gain)
    query_heads, key_heads, value_heads = (
        lax.all_to_all(query_normed, "ulysses", split_axis=1, concat_axis=0, tiled=True),
        lax.all_to_all(key_normed, "ulysses", split_axis=1, concat_axis=0, tiled=True),
        lax.all_to_all(value_proj, "ulysses", split_axis=1, concat_axis=0, tiled=True),
    )
    fold, start_state = make_fold(query_heads)
    state = fold(
        start_state,
        (
            lax.all_gather(key_heads, "blk", axis=0, tiled=True),
            lax.all_gather(value_heads, "blk", axis=0, tiled=True),
        ),
        jnp.int32(0),
    )
    attended = lax.all_to_all(finish(state), "ulysses", split_axis=0, concat_axis=1, tiled=True)
    owners = lax.axis_size("ulysses")
    tok_rows = control.shape[0]
    slab_rows = tok_rows // owners
    positions = jnp.arange(owners, dtype=jnp.int32)
    match = (owner_map[0][:, None] == positions[None, :]).astype(jnp.int32)
    inverse = jnp.sum(positions[:, None] * match, axis=0)
    gain_row = lax.dynamic_index_in_dim(hint_gain, layer_index[0], 0, keepdims=False)
    outgoing = jnp.take(control.reshape(owners, slab_rows, control.shape[1]), inverse, axis=0)
    arrived = lax.all_to_all(outgoing, "ulysses", split_axis=0, concat_axis=0, tiled=True).reshape(
        tok_rows, control.shape[1]
    )
    placed = make_hint(arrived, hint_weight)
    return (attended.astype(jnp.float32) + placed.astype(jnp.float32) * gain_row).astype(
        jnp.bfloat16
    )


def row_scale(values):
    return lax.rsqrt(jnp.mean(values * values, axis=-1, keepdims=True) + 1e-06)


def kernel(
    blks,
    owners,
    query_hbm,
    key_hbm,
    value_hbm,
    query_gain_hbm,
    key_gain_hbm,
    control_hbm,
    weight_hbm,
    gain_hbm,
    owner_hbm,
    layer_smem,
    out_ref,
    query_in,
    key_in,
    query_gain,
    key_gain,
    control_in,
    weight,
    gains,
    owner_smem,
    stage,
    landed,
    slabs_out,
    slabs_in,
    mixed_out,
    attended,
    hint,
    load_sem,
    value_sem,
    send_sem,
    recv_sem,
    slab_send,
    slab_recv,
    back_send,
    back_recv,
    far_sem,
    line_sem,
):
    rows = query_in.shape[0]
    low, high = host_range(owners)
    wide = high - low
    heads = blks * wide
    cols = blks // CORES
    devices = blks * owners
    slab_rows = rows // owners
    b = lax.axis_index("blk")
    u = lax.axis_index("ulysses")
    x = b // CORES
    me = b * owners + u
    own = b * wide + u - low
    hosting = (u >= low) & (u < high)
    visiting = jnp.logical_not(hosting)
    first_plane = u == 0
    last_plane = u == owners - 1
    leading = u == low
    near_low = 2 * u < owners
    near = jnp.where(near_low, low, high - 1)
    far = jnp.where(near_low, high - 1, low)
    partner = {"blk": x * CORES + (1 - lax.rem(b, CORES))}

    def signal(semaphore, device):
        pl.semaphore_signal(semaphore, inc=1, device_id=device, device_id_type=MESH)

    barrier = pltpu.get_barrier_semaphore()
    @pl.when(hosting)
    def _():
        for to_u in range(owners - 1, -1, -1):
            for to_b in range(blks):
                told = (to_b != b) | (u != to_u)
                if to_u == 0:
                    told = leading

                @pl.when(told)
                def _():
                    signal(barrier, {"blk": to_b, "ulysses": to_u})

    @pl.when(first_plane)
    def _():
        signal(barrier, {"ulysses": low})

    loads = [
        pltpu.make_async_copy(source, target, load_sem.at[at])
        for at, (source, target) in enumerate(
            (
                (query_hbm, query_in),
                (query_gain_hbm, query_gain),
                (key_hbm, key_in),
                (key_gain_hbm, key_gain),
                (control_hbm, control_in),
                (owner_hbm, owner_smem),
                (weight_hbm, weight),
                (gain_hbm, gains),
            )
        )
    ]
    for load in loads:
        load.start()

    def remote(source, target, sem_out, sem_in, device):
        return pltpu.make_async_remote_copy(
            src_ref=source,
            dst_ref=target,
            send_sem=sem_out,
            recv_sem=sem_in,
            device_id=device,
            device_id_type=MESH,
        )

    def drain(target, semaphore):
        pltpu.make_async_copy(target, target, semaphore).wait()

    values_at, normed_at = pl.ds(2 * rows, rows), pl.ds(0, 2 * rows)

    def columns_of(h):
        return pl.ds(pl.multiple_of(h * HEAD_DIM, HEAD_DIM), HEAD_DIM)

    def send(source, span, core, to_u):
        for aside in (*range(1, cols), 0):
            to_b = lax.rem(x + aside, cols) * CORES + core

            @pl.when((to_b != b) | (to_u != u))
            def _():
                h = to_b * wide + to_u - low
                remote(
                    source(h),
                    landed.at[me, span],
                    send_sem,
                    recv_sem,
                    {"blk": to_b, "ulysses": to_u},
                ).start()

    def send_values(to_u):
        for core in range(CORES):
            send(lambda h: value_hbm.at[:, columns_of(h)], values_at, core, to_u)

    own_values = pltpu.make_async_copy(
        value_hbm.at[:, columns_of(jnp.where(hosting, own, 0))],
        landed.at[me, values_at],
        value_sem,
    )

    @pl.when(hosting)
    def _():
        own_values.start()

    @pl.when(first_plane)
    def _():
        pl.semaphore_wait(barrier, blks)
        send_values(near)

    @pl.when(jnp.logical_not(first_plane))
    def _():
        pl.semaphore_wait(barrier, heads - hosting.astype(jnp.int32) + leading.astype(jnp.int32))

        @pl.when(leading)
        def _():
            signal(far_sem, {"ulysses": 0})
            signal(line_sem, {"ulysses": far})

        @pl.when(last_plane)
        def _():
            for to_u in range(low, high):
                signal(far_sem, {"ulysses": to_u})

        send_values(far)
        send_values(near)

    for load in loads[:4]:
        load.wait()
    for first, gain, part in ((query_in, query_gain, 0), (key_in, key_gain, 1)):
        values = first[...].astype(jnp.float32)
        normed = (values * row_scale(values) * gain[...]).astype(jnp.bfloat16)
        for h in range(heads):
            stage[h, part * rows : (part + 1) * rows] = normed[
                :, h * HEAD_DIM : (h + 1) * HEAD_DIM
            ]

    def send_normed(core, to_u):
        send(lambda h: stage.at[h], normed_at, core, to_u)

    @pl.when(first_plane)
    def _():
        send_normed(0, near)
        pl.semaphore_wait(far_sem, 1)
        send_values(far)
        send_normed(0, far)

    @pl.when(jnp.logical_not(first_plane))
    def _():
        send_normed(0, far)
        send_normed(0, near)

    for core in range(1, CORES):
        send_normed(core, far)
        send_normed(core, near)

    loads[4].wait()
    loads[5].wait()
    values = control_in[...].astype(jnp.float32)
    normed = values * row_scale(values)
    pieces = [normed[j * slab_rows : (j + 1) * slab_rows] for j in range(owners)]
    for to in range(owners):
        picked = pieces[0]
        for j in range(1, owners):
            picked = jnp.where(owner_smem[0, j] == to, pieces[j], picked)
        slabs_out[to] = picked.astype(jnp.bfloat16)

    @pl.when(hosting)
    def _():
        pl.semaphore_wait(far_sem, 1)

    @pl.when(leading)
    def _():
        for to_u in (0, owners - 1):
            signal(line_sem, {"ulysses": to_u})

    @pl.when(jnp.logical_not(leading))
    def _():
        pl.semaphore_wait(line_sem, 1)

    for d in range(1, owners):
        there = lax.rem(u + d, owners)
        remote(
            slabs_out.at[there], slabs_in.at[u], slab_send, slab_recv, {"ulysses": there}
        ).start()
    slabs_in[u] = slabs_out[u]

    order = [
        (to_b, to_u)
        for to_u in sorted(range(owners), key=lambda at: (low <= at < high, at))
        for to_b in range(blks)
    ]
    factor = HEAD_DIM ** (-0.5) * math.log2(math.e)

    @pl.when(hosting)
    def _():
        landed[me, normed_at] = stage[own]
        own_values.wait()
        drain(landed.at[pl.ds(0, devices - 1)], recv_sem)

        count = devices * rows
        keys = landed[:, rows : 2 * rows].reshape(count, HEAD_DIM)
        mix = landed[:, 2 * rows :].reshape(count, HEAD_DIM)
        group = devices // GROUPS

        def flush(base):
            for to_b, to_u in order[base : base + group]:
                there = to_b * owners + to_u

                @pl.when(there != me)
                def _():
                    remote(
                        mixed_out.at[there],
                        attended.at[own],
                        back_send,
                        back_recv,
                        {"blk": to_b, "ulysses": to_u},
                    ).start()

        for base in range(0, devices, group):
            part = [to_b * owners + to_u for to_b, to_u in order[base : base + group]]
            queries = jnp.concatenate([landed[there, :rows] for there in part], axis=0)
            scores = lax.dot_general(
                queries, keys, (((1,), (1,)), ((), ())), preferred_element_type=jnp.float32
            )
            peak = jnp.max(scores, axis=-1, keepdims=True)
            expo = jnp.exp2((scores - peak) * factor)
            totals = jnp.sum(expo, axis=-1, keepdims=True)
            output = jnp.dot(
                expo.astype(jnp.bfloat16), mix, preferred_element_type=jnp.float32
            )
            output = (output * (1.0 / totals)).astype(jnp.bfloat16)
            for at, there in enumerate(part):
                mixed_out[there] = output[at * rows : (at + 1) * rows]
            flush(base)
        attended[own] = mixed_out[me]

    loads[6].wait()
    loads[7].wait()
    drain(slabs_in.at[pl.ds(0, owners - 1)], slab_recv)
    arrived = slabs_in[...].astype(jnp.float32).reshape(rows, control_in.shape[1])
    placed = jnp.dot(
        arrived.astype(jnp.bfloat16), weight[...], preferred_element_type=jnp.float32
    ).astype(jnp.bfloat16)
    hint[...] = placed.astype(jnp.float32) * gains[pl.ds(layer_smem[0], 1), :]
    drain(slabs_in.at[pl.ds(0, owners - 1)], slab_send)

    @pl.when(hosting)
    def _():
        drain(landed.at[pl.ds(0, heads - 1)], send_sem)
        drain(mixed_out.at[pl.ds(0, devices - 1)], back_send)
        drain(attended.at[pl.ds(0, heads - 1)], back_recv)

    @pl.when(visiting)
    def _():
        drain(landed.at[pl.ds(0, heads)], send_sem)
        drain(attended, back_recv)

    for h in range(heads):
        columns = slice(h * HEAD_DIM, (h + 1) * HEAD_DIM)
        out_ref[:, columns] = (attended[h].astype(jnp.float32) + hint[:, columns]).astype(
            jnp.bfloat16
        )


GROUPS = 4


def host_range(owners):
    low = owners // 4
    return (low, owners - low)


def run(blks, owners, *arrays):
    query_proj, control, hint_weight, hint_gain = arrays[0], arrays[5], arrays[6], arrays[7]
    rows, feats = query_proj.shape
    low, high = host_range(owners)
    heads = blks * (high - low)
    devices = blks * owners
    fits = (
        blks % CORES == 0
        and owners > 1
        and heads * HEAD_DIM == feats
        and (low, high) == (1, owners - 1)
        and high - low == 2
        and devices % GROUPS == 0
        and rows % 16 == 0
        and rows % owners == 0
        and (rows // owners) % 8 == 0
        and rows * devices <= 1024
    )
    if not fits:
        return shards(*arrays)
    inner = control.shape[1]
    dma = pltpu.SemaphoreType.DMA
    half = jnp.bfloat16
    wide = jnp.float32
    operands = list(arrays)
    operands[3] = arrays[3].reshape(1, feats)
    operands[4] = arrays[4].reshape(1, feats)
    layer = operands.pop()
    operands = [pltpu.with_memory_space_constraint(array, pltpu.HBM) for array in operands]
    return pl.pallas_call(
        functools.partial(kernel, blks, owners),
        out_shape=jax.ShapeDtypeStruct((rows, feats), half),
        in_specs=[pl.BlockSpec(memory_space=pltpu.HBM)] * len(operands)
        + [pl.BlockSpec(memory_space=pltpu.SMEM)],
        out_specs=pl.BlockSpec(memory_space=pltpu.VMEM),
        scratch_shapes=[
            pltpu.VMEM((rows, feats), half),
            pltpu.VMEM((rows, feats), half),
            pltpu.VMEM((1, feats), wide),
            pltpu.VMEM((1, feats), wide),
            pltpu.VMEM((rows, inner), half),
            pltpu.VMEM(hint_weight.shape, half),
            pltpu.VMEM(hint_gain.shape, wide),
            pltpu.SMEM((1, owners), jnp.int32),
            pltpu.VMEM((heads, 2 * rows, HEAD_DIM), half),
            pltpu.VMEM((devices, 3 * rows, HEAD_DIM), half),
            pltpu.VMEM((owners, rows // owners, inner), half),
            pltpu.VMEM((owners, rows // owners, inner), half),
            pltpu.VMEM((devices, rows, HEAD_DIM), half),
            pltpu.VMEM((heads, rows, HEAD_DIM), half),
            pltpu.VMEM((rows, feats), wide),
            dma((len(operands),)),
            dma,
            dma,
            dma,
            dma,
            dma,
            dma,
            dma,
            pltpu.SemaphoreType.REGULAR,
            pltpu.SemaphoreType.REGULAR,
        ],
        compiler_params=pltpu.CompilerParams(
            collective_id=0, has_side_effects=True, vmem_limit_bytes=16 << 20
        ),
    )(*operands, layer)


def solution(mesh):
    return jax.shard_map(
        functools.partial(run, mesh.shape["blk"], mesh.shape["ulysses"]),
        mesh=mesh,
        in_specs=(
            P(("groups", "blk", "ulysses"), None),
            P(("groups", "blk", "ulysses"), None),
            P(("groups", "blk", "ulysses"), None),
            P(),
            P(),
            P(("groups", "blk", "ulysses"), None),
            P(),
            P(),
            P(("groups", "blk", "ulysses"), None),
            P(("groups", "blk", "ulysses")),
        ),
        out_specs=P(("groups", "blk", "ulysses"), None),
        check_vma=False,
    )
```

```python
import functools
import math

import jax
import jax.numpy as jnp
from jax import lax
from jax.experimental import pallas as pl
from jax.experimental.pallas import tpu as pltpu
from jax.sharding import PartitionSpec as P

HEAD_DIM = 128
CORES = 2
MESH = pl.DeviceIdType.MESH


def normalize_rows(rows, gain):
    values = rows.astype(jnp.float32)
    scale = lax.rsqrt(jnp.mean(values * values, axis=-1, keepdims=True) + 1e-06)
    return (values * scale * gain).astype(jnp.bfloat16)


def block_size(count):
    block = min(count, 1024)
    while count % block:
        block = block - 1
    return block


def make_fold(queries):
    rows = queries.shape[0]
    heads = queries.shape[1] // HEAD_DIM
    shaped = queries.reshape(rows, heads, HEAD_DIM)
    factor = HEAD_DIM ** (-0.5)

    def update(state, pair):
        peak, totals, accum = state
        key_block, value_block = pair
        scores = (
            jnp.einsum("qhd,khd->hqk", shaped, key_block, preferred_element_type=jnp.float32)
            * factor
        )
        new_peak = jnp.maximum(peak, jnp.max(scores, axis=-1))
        correction = jnp.exp(peak - new_peak)
        expo = jnp.exp(scores - new_peak[:, :, None])
        totals = totals * correction + jnp.sum(expo, axis=-1)
        mixed = jnp.einsum(
            "hqk,khd->hqd",
            expo.astype(jnp.bfloat16),
            value_block,
            preferred_element_type=jnp.float32,
        )
        accum = accum * correction[:, :, None] + mixed
        return ((new_peak, totals, accum), None)

    def fold(carry, piece, start):
        keys, values = piece
        count = keys.shape[0]
        block = block_size(count)
        key_blocks = keys.reshape(count // block, block, heads, HEAD_DIM)
        value_blocks = values.reshape(count // block, block, heads, HEAD_DIM)
        result, unused = lax.scan(update, carry, (key_blocks, value_blocks))
        return result

    start_state = (
        jnp.full((heads, rows), -1e30, jnp.float32),
        jnp.zeros((heads, rows), jnp.float32),
        jnp.zeros((heads, rows, HEAD_DIM), jnp.float32),
    )
    return (fold, start_state)


def finish(state):
    peak, totals, accum = state
    heads, rows = totals.shape
    output = (accum / totals[:, :, None]).astype(jnp.bfloat16)
    return output.transpose(1, 0, 2).reshape(rows, heads * HEAD_DIM)


def make_hint(patches, hint_weight):
    normed = normalize_rows(patches, jnp.float32(1.0))
    return jnp.dot(normed, hint_weight, preferred_element_type=jnp.float32).astype(jnp.bfloat16)


def shards(
    query_proj,
    key_proj,
    value_proj,
    query_gain,
    key_gain,
    control,
    hint_weight,
    hint_gain,
    owner_map,
    layer_index,
):
    query_normed = normalize_rows(query_proj, query_gain)
    key_normed = normalize_rows(key_proj, key_gain)
    query_heads, key_heads, value_heads = (
        lax.all_to_all(query_normed, "ulysses", split_axis=1, concat_axis=0, tiled=True),
        lax.all_to_all(key_normed, "ulysses", split_axis=1, concat_axis=0, tiled=True),
        lax.all_to_all(value_proj, "ulysses", split_axis=1, concat_axis=0, tiled=True),
    )
    fold, start_state = make_fold(query_heads)
    state = fold(
        start_state,
        (
            lax.all_gather(key_heads, "blk", axis=0, tiled=True),
            lax.all_gather(value_heads, "blk", axis=0, tiled=True),
        ),
        jnp.int32(0),
    )
    attended = lax.all_to_all(finish(state), "ulysses", split_axis=0, concat_axis=1, tiled=True)
    owners = lax.axis_size("ulysses")
    tok_rows = control.shape[0]
    slab_rows = tok_rows // owners
    positions = jnp.arange(owners, dtype=jnp.int32)
    match = (owner_map[0][:, None] == positions[None, :]).astype(jnp.int32)
    inverse = jnp.sum(positions[:, None] * match, axis=0)
    gain_row = lax.dynamic_index_in_dim(hint_gain, layer_index[0], 0, keepdims=False)
    outgoing = jnp.take(control.reshape(owners, slab_rows, control.shape[1]), inverse, axis=0)
    arrived = lax.all_to_all(outgoing, "ulysses", split_axis=0, concat_axis=0, tiled=True).reshape(
        tok_rows, control.shape[1]
    )
    placed = make_hint(arrived, hint_weight)
    return (attended.astype(jnp.float32) + placed.astype(jnp.float32) * gain_row).astype(
        jnp.bfloat16
    )


def row_scale(values):
    return lax.rsqrt(jnp.mean(values * values, axis=-1, keepdims=True) + 1e-06)


def kernel(
    blks,
    owners,
    query_hbm,
    key_hbm,
    value_hbm,
    query_gain_hbm,
    key_gain_hbm,
    control_hbm,
    weight_hbm,
    gain_hbm,
    owner_hbm,
    layer_smem,
    out_ref,
    query_in,
    key_in,
    query_gain,
    key_gain,
    control_in,
    weight,
    gains,
    owner_smem,
    stage,
    landed,
    slabs_out,
    slabs_in,
    mixed_out,
    attended,
    hint,
    load_sem,
    value_sem,
    send_sem,
    recv_sem,
    query_sem,
    slab_send,
    slab_recv,
    back_send,
    back_recv,
    far_sem,
    line_sem,
):
    rows = query_in.shape[0]
    low, high = host_range(owners)
    wide = high - low
    heads = blks * wide
    cols = blks // CORES
    devices = blks * owners
    slab_rows = rows // owners
    b = lax.axis_index("blk")
    u = lax.axis_index("ulysses")
    x = b // CORES
    me = b * owners + u
    own = b * wide + u - low
    hosting = (u >= low) & (u < high)
    visiting = jnp.logical_not(hosting)
    first_plane = u == 0
    last_plane = u == owners - 1
    leading = u == low
    near_low = 2 * u < owners
    near = jnp.where(near_low, low, high - 1)
    far = jnp.where(near_low, high - 1, low)
    partner = {"blk": x * CORES + (1 - lax.rem(b, CORES))}

    def signal(semaphore, device):
        pl.semaphore_signal(semaphore, inc=1, device_id=device, device_id_type=MESH)

    barrier = pltpu.get_barrier_semaphore()
    @pl.when(hosting)
    def _():
        for to_u in range(owners - 1, -1, -1):
            for to_b in range(blks):
                told = (to_b != b) | (u != to_u)
                if to_u == 0:
                    told = leading

                @pl.when(told)
                def _():
                    signal(barrier, {"blk": to_b, "ulysses": to_u})

    @pl.when(first_plane)
    def _():
        signal(barrier, {"ulysses": low})

    loads = [
        pltpu.make_async_copy(source, target, load_sem.at[at])
        for at, (source, target) in enumerate(
            (
                (query_hbm, query_in),
                (query_gain_hbm, query_gain),
                (key_hbm, key_in),
                (key_gain_hbm, key_gain),
                (control_hbm, control_in),
                (owner_hbm, owner_smem),
                (weight_hbm, weight),
                (gain_hbm, gains),
            )
        )
    ]
    for load in loads:
        load.start()

    def remote(source, target, sem_out, sem_in, device):
        return pltpu.make_async_remote_copy(
            src_ref=source,
            dst_ref=target,
            send_sem=sem_out,
            recv_sem=sem_in,
            device_id=device,
            device_id_type=MESH,
        )

    def drain(target, semaphore):
        pltpu.make_async_copy(target, target, semaphore).wait()

    queries_at, keys_at, values_at = (pl.ds(at * rows, rows) for at in range(3))
    early = jnp.where(first_plane, 0, 1)

    def columns_of(h):
        return pl.ds(pl.multiple_of(h * HEAD_DIM, HEAD_DIM), HEAD_DIM)

    def send(source, span, semaphore, core, to_u):
        for aside in (*range(1, cols), 0):
            to_b = lax.rem(x + aside, cols) * CORES + core

            @pl.when((to_b != b) | (to_u != u))
            def _():
                h = to_b * wide + to_u - low
                remote(
                    source(h),
                    landed.at[me, span],
                    send_sem,
                    semaphore,
                    {"blk": to_b, "ulysses": to_u},
                ).start()

    def send_values(core, to_u):
        send(lambda h: value_hbm.at[:, columns_of(h)], values_at, recv_sem, core, to_u)

    own_values = pltpu.make_async_copy(
        value_hbm.at[:, columns_of(jnp.where(hosting, own, 0))],
        landed.at[me, values_at],
        value_sem,
    )

    @pl.when(hosting)
    def _():
        own_values.start()

    @pl.when(first_plane)
    def _():
        pl.semaphore_wait(barrier, blks)
        send_values(0, near)

    @pl.when(jnp.logical_not(first_plane))
    def _():
        pl.semaphore_wait(barrier, heads - hosting.astype(jnp.int32) + leading.astype(jnp.int32))

        @pl.when(leading)
        def _():
            signal(far_sem, {"ulysses": 0})
            signal(line_sem, {"ulysses": far})

        @pl.when(last_plane)
        def _():
            for to_u in range(low, high):
                signal(far_sem, {"ulysses": to_u})

        for to_u in (far, near):
            for core in range(CORES):
                send_values(core, to_u)

    for load in loads[:4]:
        load.wait()
    for first, gain, part in ((query_in, query_gain, 0), (key_in, key_gain, 1)):
        values = first[...].astype(jnp.float32)
        normed = (values * row_scale(values) * gain[...]).astype(jnp.bfloat16)
        for h in range(heads):
            stage[h, part * rows : (part + 1) * rows] = normed[
                :, h * HEAD_DIM : (h + 1) * HEAD_DIM
            ]

    def send_keys(core, to_u):
        send(lambda h: stage.at[h, keys_at], keys_at, recv_sem, core, to_u)

    def send_queries(core, to_u):
        send(lambda h: stage.at[h, queries_at], queries_at, query_sem.at[early], core, to_u)

    @pl.when(first_plane)
    def _():
        send_keys(0, near)
        send_queries(0, near)
        send_values(1, near)
        pl.semaphore_wait(far_sem, 1)
        for core in range(CORES):
            send_values(core, far)
            send_keys(core, far)
            send_queries(core, far)
        for core in range(1, CORES):
            send_keys(core, near)
            send_queries(core, near)

    @pl.when(jnp.logical_not(first_plane))
    def _():
        for part in (send_keys, send_queries):
            for core in range(CORES):
                part(core, far)
                part(core, near)

    loads[4].wait()
    loads[5].wait()
    values = control_in[...].astype(jnp.float32)
    normed = values * row_scale(values)
    pieces = [normed[j * slab_rows : (j + 1) * slab_rows] for j in range(owners)]
    for to in range(owners):
        picked = pieces[0]
        for j in range(1, owners):
            picked = jnp.where(owner_smem[0, j] == to, pieces[j], picked)
        slabs_out[to] = picked.astype(jnp.bfloat16)

    @pl.when(hosting)
    def _():
        pl.semaphore_wait(far_sem, 1)

    @pl.when(leading)
    def _():
        for to_u in (0, owners - 1):
            signal(line_sem, {"ulysses": to_u})

    @pl.when(jnp.logical_not(leading))
    def _():
        pl.semaphore_wait(line_sem, 1)

    for d in range(1, owners):
        there = lax.rem(u + d, owners)
        remote(
            slabs_out.at[there], slabs_in.at[u], slab_send, slab_recv, {"ulysses": there}
        ).start()
    slabs_in[u] = slabs_out[u]

    order = [
        (to_b, to_u)
        for to_u in sorted(range(owners), key=lambda at: (low <= at < high, at))
        for to_b in range(blks)
    ]
    factor = HEAD_DIM ** (-0.5) * math.log2(math.e)

    @pl.when(hosting)
    def _():
        landed[me, 0 : 2 * rows] = stage[own]
        own_values.wait()
        drain(landed.at[pl.ds(0, devices - 1), pl.ds(0, 2 * rows)], recv_sem)
        drain(landed.at[pl.ds(0, blks), queries_at], query_sem.at[0])

        count = devices * rows
        keys = landed[:, rows : 2 * rows].reshape(count, HEAD_DIM)
        mix = landed[:, 2 * rows :].reshape(count, HEAD_DIM)
        group = blks

        def flush(base):
            for to_b, to_u in order[base : base + group]:
                there = to_b * owners + to_u

                @pl.when(there != me)
                def _():
                    remote(
                        mixed_out.at[there],
                        attended.at[own],
                        back_send,
                        back_recv,
                        {"blk": to_b, "ulysses": to_u},
                    ).start()

        for base in range(0, devices, group):
            if base == group:
                drain(landed.at[pl.ds(0, devices - blks - 1), queries_at], query_sem.at[1])
            part = [to_b * owners + to_u for to_b, to_u in order[base : base + group]]
            queries = jnp.concatenate([landed[there, :rows] for there in part], axis=0)
            scores = lax.dot_general(
                queries, keys, (((1,), (1,)), ((), ())), preferred_element_type=jnp.float32
            )
            peak = jnp.max(scores, axis=-1, keepdims=True)
            expo = jnp.exp2((scores - peak) * factor)
            totals = jnp.sum(expo, axis=-1, keepdims=True)
            output = jnp.dot(
                expo.astype(jnp.bfloat16), mix, preferred_element_type=jnp.float32
            )
            output = (output * (1.0 / totals)).astype(jnp.bfloat16)
            for at, there in enumerate(part):
                mixed_out[there] = output[at * rows : (at + 1) * rows]
            flush(base)
        attended[own] = mixed_out[me]

    loads[6].wait()
    loads[7].wait()
    drain(slabs_in.at[pl.ds(0, owners - 1)], slab_recv)
    arrived = slabs_in[...].astype(jnp.float32).reshape(rows, control_in.shape[1])
    placed = jnp.dot(
        arrived.astype(jnp.bfloat16), weight[...], preferred_element_type=jnp.float32
    ).astype(jnp.bfloat16)
    hint[...] = placed.astype(jnp.float32) * gains[pl.ds(layer_smem[0], 1), :]
    drain(slabs_in.at[pl.ds(0, owners - 1)], slab_send)

    @pl.when(hosting)
    def _():
        drain(landed.at[pl.ds(0, heads - 1)], send_sem)
        drain(mixed_out.at[pl.ds(0, devices - 1)], back_send)
        drain(attended.at[pl.ds(0, heads - 1)], back_recv)

    @pl.when(visiting)
    def _():
        drain(landed.at[pl.ds(0, heads)], send_sem)
        drain(attended, back_recv)

    for h in range(heads):
        columns = slice(h * HEAD_DIM, (h + 1) * HEAD_DIM)
        out_ref[:, columns] = (attended[h].astype(jnp.float32) + hint[:, columns]).astype(
            jnp.bfloat16
        )


def host_range(owners):
    low = owners // 4
    return (low, owners - low)


def run(blks, owners, *arrays):
    query_proj, control, hint_weight, hint_gain = arrays[0], arrays[5], arrays[6], arrays[7]
    rows, feats = query_proj.shape
    low, high = host_range(owners)
    heads = blks * (high - low)
    devices = blks * owners
    fits = (
        blks % CORES == 0
        and owners > 1
        and heads * HEAD_DIM == feats
        and (low, high) == (1, owners - 1)
        and high - low == 2
        and rows % 16 == 0
        and rows % owners == 0
        and (rows // owners) % 8 == 0
        and rows * devices <= 1024
    )
    if not fits:
        return shards(*arrays)
    inner = control.shape[1]
    dma = pltpu.SemaphoreType.DMA
    half = jnp.bfloat16
    wide = jnp.float32
    operands = list(arrays)
    operands[3] = arrays[3].reshape(1, feats)
    operands[4] = arrays[4].reshape(1, feats)
    layer = operands.pop()
    operands = [pltpu.with_memory_space_constraint(array, pltpu.HBM) for array in operands]
    return pl.pallas_call(
        functools.partial(kernel, blks, owners),
        out_shape=jax.ShapeDtypeStruct((rows, feats), half),
        in_specs=[pl.BlockSpec(memory_space=pltpu.HBM)] * len(operands)
        + [pl.BlockSpec(memory_space=pltpu.SMEM)],
        out_specs=pl.BlockSpec(memory_space=pltpu.VMEM),
        scratch_shapes=[
            pltpu.VMEM((rows, feats), half),
            pltpu.VMEM((rows, feats), half),
            pltpu.VMEM((1, feats), wide),
            pltpu.VMEM((1, feats), wide),
            pltpu.VMEM((rows, inner), half),
            pltpu.VMEM(hint_weight.shape, half),
            pltpu.VMEM(hint_gain.shape, wide),
            pltpu.SMEM((1, owners), jnp.int32),
            pltpu.VMEM((heads, 2 * rows, HEAD_DIM), half),
            pltpu.VMEM((devices, 3 * rows, HEAD_DIM), half),
            pltpu.VMEM((owners, rows // owners, inner), half),
            pltpu.VMEM((owners, rows // owners, inner), half),
            pltpu.VMEM((devices, rows, HEAD_DIM), half),
            pltpu.VMEM((heads, rows, HEAD_DIM), half),
            pltpu.VMEM((rows, feats), wide),
            dma((len(operands),)),
            dma,
            dma,
            dma,
            dma((2,)),
            dma,
            dma,
            dma,
            dma,
            pltpu.SemaphoreType.REGULAR,
            pltpu.SemaphoreType.REGULAR,
        ],
        compiler_params=pltpu.CompilerParams(
            collective_id=0, has_side_effects=True, vmem_limit_bytes=16 << 20
        ),
    )(*operands, layer)


def solution(mesh):
    return jax.shard_map(
        functools.partial(run, mesh.shape["blk"], mesh.shape["ulysses"]),
        mesh=mesh,
        in_specs=(
            P(("groups", "blk", "ulysses"), None),
            P(("groups", "blk", "ulysses"), None),
            P(("groups", "blk", "ulysses"), None),
            P(),
            P(),
            P(("groups", "blk", "ulysses"), None),
            P(),
            P(),
            P(("groups", "blk", "ulysses"), None),
            P(("groups", "blk", "ulysses")),
        ),
        out_specs=P(("groups", "blk", "ulysses"), None),
        check_vma=False,
    )
```

```python
import functools
import math

import jax
import jax.numpy as jnp
from jax import lax
from jax.experimental import pallas as pl
from jax.experimental.pallas import tpu as pltpu
from jax.sharding import PartitionSpec as P

HEAD_DIM = 128
CORES = 2
MESH = pl.DeviceIdType.MESH


def normalize_rows(rows, gain):
    values = rows.astype(jnp.float32)
    scale = lax.rsqrt(jnp.mean(values * values, axis=-1, keepdims=True) + 1e-06)
    return (values * scale * gain).astype(jnp.bfloat16)


def block_size(count):
    block = min(count, 1024)
    while count % block:
        block = block - 1
    return block


def make_fold(queries):
    rows = queries.shape[0]
    heads = queries.shape[1] // HEAD_DIM
    shaped = queries.reshape(rows, heads, HEAD_DIM)
    factor = HEAD_DIM ** (-0.5)

    def update(state, pair):
        peak, totals, accum = state
        key_block, value_block = pair
        scores = (
            jnp.einsum("qhd,khd->hqk", shaped, key_block, preferred_element_type=jnp.float32)
            * factor
        )
        new_peak = jnp.maximum(peak, jnp.max(scores, axis=-1))
        correction = jnp.exp(peak - new_peak)
        expo = jnp.exp(scores - new_peak[:, :, None])
        totals = totals * correction + jnp.sum(expo, axis=-1)
        mixed = jnp.einsum(
            "hqk,khd->hqd",
            expo.astype(jnp.bfloat16),
            value_block,
            preferred_element_type=jnp.float32,
        )
        accum = accum * correction[:, :, None] + mixed
        return ((new_peak, totals, accum), None)

    def fold(carry, piece, start):
        keys, values = piece
        count = keys.shape[0]
        block = block_size(count)
        key_blocks = keys.reshape(count // block, block, heads, HEAD_DIM)
        value_blocks = values.reshape(count // block, block, heads, HEAD_DIM)
        result, unused = lax.scan(update, carry, (key_blocks, value_blocks))
        return result

    start_state = (
        jnp.full((heads, rows), -1e30, jnp.float32),
        jnp.zeros((heads, rows), jnp.float32),
        jnp.zeros((heads, rows, HEAD_DIM), jnp.float32),
    )
    return (fold, start_state)


def finish(state):
    peak, totals, accum = state
    heads, rows = totals.shape
    output = (accum / totals[:, :, None]).astype(jnp.bfloat16)
    return output.transpose(1, 0, 2).reshape(rows, heads * HEAD_DIM)


def make_hint(patches, hint_weight):
    normed = normalize_rows(patches, jnp.float32(1.0))
    return jnp.dot(normed, hint_weight, preferred_element_type=jnp.float32).astype(jnp.bfloat16)


def shards(
    query_proj,
    key_proj,
    value_proj,
    query_gain,
    key_gain,
    control,
    hint_weight,
    hint_gain,
    owner_map,
    layer_index,
):
    query_normed = normalize_rows(query_proj, query_gain)
    key_normed = normalize_rows(key_proj, key_gain)
    query_heads, key_heads, value_heads = (
        lax.all_to_all(query_normed, "ulysses", split_axis=1, concat_axis=0, tiled=True),
        lax.all_to_all(key_normed, "ulysses", split_axis=1, concat_axis=0, tiled=True),
        lax.all_to_all(value_proj, "ulysses", split_axis=1, concat_axis=0, tiled=True),
    )
    fold, start_state = make_fold(query_heads)
    state = fold(
        start_state,
        (
            lax.all_gather(key_heads, "blk", axis=0, tiled=True),
            lax.all_gather(value_heads, "blk", axis=0, tiled=True),
        ),
        jnp.int32(0),
    )
    attended = lax.all_to_all(finish(state), "ulysses", split_axis=0, concat_axis=1, tiled=True)
    owners = lax.axis_size("ulysses")
    tok_rows = control.shape[0]
    slab_rows = tok_rows // owners
    positions = jnp.arange(owners, dtype=jnp.int32)
    match = (owner_map[0][:, None] == positions[None, :]).astype(jnp.int32)
    inverse = jnp.sum(positions[:, None] * match, axis=0)
    gain_row = lax.dynamic_index_in_dim(hint_gain, layer_index[0], 0, keepdims=False)
    outgoing = jnp.take(control.reshape(owners, slab_rows, control.shape[1]), inverse, axis=0)
    arrived = lax.all_to_all(outgoing, "ulysses", split_axis=0, concat_axis=0, tiled=True).reshape(
        tok_rows, control.shape[1]
    )
    placed = make_hint(arrived, hint_weight)
    return (attended.astype(jnp.float32) + placed.astype(jnp.float32) * gain_row).astype(
        jnp.bfloat16
    )


def row_scale(values):
    return lax.rsqrt(jnp.mean(values * values, axis=-1, keepdims=True) + 1e-06)


def kernel(
    blks,
    owners,
    query_hbm,
    key_hbm,
    value_hbm,
    query_gain_hbm,
    key_gain_hbm,
    control_hbm,
    weight_hbm,
    gain_hbm,
    owner_hbm,
    layer_smem,
    out_ref,
    query_in,
    key_in,
    query_gain,
    key_gain,
    control_in,
    weight,
    gains,
    owner_smem,
    stage,
    landed,
    slabs_out,
    slabs_in,
    mixed_out,
    attended,
    hint,
    load_sem,
    value_sem,
    send_sem,
    recv_sem,
    query_sem,
    slab_send,
    slab_recv,
    back_send,
    back_recv,
    far_sem,
    line_sem,
):
    rows = query_in.shape[0]
    low, high = host_range(owners)
    wide = high - low
    heads = blks * wide
    cols = blks // CORES
    devices = blks * owners
    slab_rows = rows // owners
    b = lax.axis_index("blk")
    u = lax.axis_index("ulysses")
    x = b // CORES
    me = b * owners + u
    own = b * wide + u - low
    hosting = (u >= low) & (u < high)
    visiting = jnp.logical_not(hosting)
    first_plane = u == 0
    last_plane = u == owners - 1
    leading = u == low
    near_low = 2 * u < owners
    near = jnp.where(near_low, low, high - 1)
    far = jnp.where(near_low, high - 1, low)
    partner = {"blk": x * CORES + (1 - lax.rem(b, CORES))}

    def signal(semaphore, device):
        pl.semaphore_signal(semaphore, inc=1, device_id=device, device_id_type=MESH)

    barrier = pltpu.get_barrier_semaphore()
    @pl.when(hosting)
    def _():
        for to_b in range(blks):
            signal(barrier, {"blk": to_b, "ulysses": far})

        @pl.when(leading)
        def _():
            for to_b in range(blks):
                signal(barrier, {"blk": to_b, "ulysses": 0})

        for to_b in range(blks):
            signal(barrier, {"blk": to_b, "ulysses": owners - 1})
        for step in range(1, blks):
            signal(barrier, {"blk": lax.rem(b + step, blks)})

    @pl.when(first_plane)
    def _():
        signal(barrier, {"ulysses": low})

    loads = [
        pltpu.make_async_copy(source, target, load_sem.at[at])
        for at, (source, target) in enumerate(
            (
                (query_hbm, query_in),
                (query_gain_hbm, query_gain),
                (key_hbm, key_in),
                (key_gain_hbm, key_gain),
                (control_hbm, control_in),
                (owner_hbm, owner_smem),
                (weight_hbm, weight),
                (gain_hbm, gains),
            )
        )
    ]
    for load in loads:
        load.start()

    def remote(source, target, sem_out, sem_in, device):
        return pltpu.make_async_remote_copy(
            src_ref=source,
            dst_ref=target,
            send_sem=sem_out,
            recv_sem=sem_in,
            device_id=device,
            device_id_type=MESH,
        )

    def drain(target, semaphore):
        pltpu.make_async_copy(target, target, semaphore).wait()

    queries_at, keys_at, values_at = (pl.ds(at * rows, rows) for at in range(3))
    early = jnp.where(first_plane, 0, 1)

    def columns_of(h):
        return pl.ds(pl.multiple_of(h * HEAD_DIM, HEAD_DIM), HEAD_DIM)

    def send(source, span, semaphore, core, to_u, columns=None):
        for to_x in range(cols - 1, -1, -1) if columns is None else columns:
            to_b = to_x * CORES + core

            @pl.when((to_b != b) | (to_u != u))
            def _():
                h = to_b * wide + to_u - low
                remote(
                    source(h),
                    landed.at[me, span],
                    send_sem,
                    semaphore,
                    {"blk": to_b, "ulysses": to_u},
                ).start()

    def send_values(core, to_u, *asides):
        send(lambda h: value_hbm.at[:, columns_of(h)], values_at, recv_sem, core, to_u, *asides)

    own_values = pltpu.make_async_copy(
        value_hbm.at[:, columns_of(jnp.where(hosting, own, 0))],
        landed.at[me, values_at],
        value_sem,
    )

    @pl.when(hosting)
    def _():
        own_values.start()

    @pl.when(first_plane)
    def _():
        pl.semaphore_wait(barrier, blks)
        send_values(0, near, (cols - 1,))
        send_values(1, near, (cols - 1,))

    @pl.when(jnp.logical_not(first_plane))
    def _():
        pl.semaphore_wait(barrier, heads - hosting.astype(jnp.int32) + leading.astype(jnp.int32))

        @pl.when(leading)
        def _():
            signal(far_sem, {"ulysses": 0})
            signal(line_sem, {"ulysses": far})

        @pl.when(last_plane)
        def _():
            for to_u in range(low, high):
                signal(far_sem, {"ulysses": to_u})

        for to_u in (far, near):
            for core in range(CORES):
                send_values(core, to_u)

    for load in loads[:4]:
        load.wait()
    for first, gain, part in ((query_in, query_gain, 0), (key_in, key_gain, 1)):
        values = first[...].astype(jnp.float32)
        normed = (values * row_scale(values) * gain[...]).astype(jnp.bfloat16)
        for h in range(heads):
            stage[h, part * rows : (part + 1) * rows] = normed[
                :, h * HEAD_DIM : (h + 1) * HEAD_DIM
            ]

    def send_keys(core, to_u, *asides):
        send(lambda h: stage.at[h, keys_at], keys_at, recv_sem, core, to_u, *asides)

    def send_queries(core, to_u, *asides):
        send(lambda h: stage.at[h, queries_at], queries_at, query_sem.at[early], core, to_u, *asides)

    @pl.when(first_plane)
    def _():
        def bundle(core, to_u, to_x):
            send_values(core, to_u, (to_x,))
            send_keys(core, to_u, (to_x,))
            send_queries(core, to_u, (to_x,))

        def normed_pair(core, to_u, to_x):
            send_keys(core, to_u, (to_x,))
            send_queries(core, to_u, (to_x,))

        last = cols - 1
        normed_pair(0, near, last)
        normed_pair(1, near, last)
        pl.semaphore_wait(far_sem, 1)
        bundle(0, far, last)
        bundle(1, far, last)
        bundle(0, far, 0)
        bundle(0, near, 0)
        bundle(1, far, 0)
        bundle(1, near, 0)

    @pl.when(jnp.logical_not(first_plane))
    def _():
        for part in (send_keys, send_queries):
            for core in range(CORES):
                part(core, far)
                part(core, near)

    loads[4].wait()
    loads[5].wait()
    values = control_in[...].astype(jnp.float32)
    normed = values * row_scale(values)
    pieces = [normed[j * slab_rows : (j + 1) * slab_rows] for j in range(owners)]
    for to in range(owners):
        picked = pieces[0]
        for j in range(1, owners):
            picked = jnp.where(owner_smem[0, j] == to, pieces[j], picked)
        slabs_out[to] = picked.astype(jnp.bfloat16)

    @pl.when(hosting)
    def _():
        pl.semaphore_wait(far_sem, 1)

    @pl.when(leading)
    def _():
        for to_u in (0, owners - 1):
            signal(line_sem, {"ulysses": to_u})

    @pl.when(jnp.logical_not(leading))
    def _():
        pl.semaphore_wait(line_sem, 1)

    for d in range(1, owners):
        there = lax.rem(u + d, owners)
        remote(
            slabs_out.at[there], slabs_in.at[u], slab_send, slab_recv, {"ulysses": there}
        ).start()
    slabs_in[u] = slabs_out[u]

    order = [
        (to_b, to_u)
        for to_u in sorted(range(owners), key=lambda at: (low <= at < high, at))
        for to_b in range(blks)
    ]
    factor = HEAD_DIM ** (-0.5) * math.log2(math.e)

    @pl.when(hosting)
    def _():
        landed[me, 0 : 2 * rows] = stage[own]
        own_values.wait()
        drain(landed.at[pl.ds(0, devices - 1), pl.ds(0, 2 * rows)], recv_sem)
        drain(landed.at[pl.ds(0, blks), queries_at], query_sem.at[0])

        count = devices * rows
        keys = landed[:, rows : 2 * rows].reshape(count, HEAD_DIM)
        mix = landed[:, 2 * rows :].reshape(count, HEAD_DIM)
        group = blks

        def flush(base):
            for to_b, to_u in order[base : base + group]:
                there = to_b * owners + to_u

                @pl.when(there != me)
                def _():
                    remote(
                        mixed_out.at[there],
                        attended.at[own],
                        back_send,
                        back_recv,
                        {"blk": to_b, "ulysses": to_u},
                    ).start()

        for base in range(0, devices, group):
            if base == group:
                drain(landed.at[pl.ds(0, devices - blks - 1), queries_at], query_sem.at[1])
            part = [to_b * owners + to_u for to_b, to_u in order[base : base + group]]
            queries = jnp.concatenate([landed[there, :rows] for there in part], axis=0)
            scores = lax.dot_general(
                queries, keys, (((1,), (1,)), ((), ())), preferred_element_type=jnp.float32
            )
            peak = jnp.max(scores, axis=-1, keepdims=True)
            expo = jnp.exp2((scores - peak) * factor)
            totals = jnp.sum(expo, axis=-1, keepdims=True)
            output = jnp.dot(
                expo.astype(jnp.bfloat16), mix, preferred_element_type=jnp.float32
            )
            output = (output * (1.0 / totals)).astype(jnp.bfloat16)
            for at, there in enumerate(part):
                mixed_out[there] = output[at * rows : (at + 1) * rows]
            flush(base)
        attended[own] = mixed_out[me]

    loads[6].wait()
    loads[7].wait()
    drain(slabs_in.at[pl.ds(0, owners - 1)], slab_recv)
    arrived = slabs_in[...].astype(jnp.float32).reshape(rows, control_in.shape[1])
    placed = jnp.dot(
        arrived.astype(jnp.bfloat16), weight[...], preferred_element_type=jnp.float32
    ).astype(jnp.bfloat16)
    hint[...] = placed.astype(jnp.float32) * gains[pl.ds(layer_smem[0], 1), :]
    drain(slabs_in.at[pl.ds(0, owners - 1)], slab_send)

    @pl.when(hosting)
    def _():
        drain(landed.at[pl.ds(0, heads - 1)], send_sem)
        drain(mixed_out.at[pl.ds(0, devices - 1)], back_send)
        drain(attended.at[pl.ds(0, heads - 1)], back_recv)

    @pl.when(visiting)
    def _():
        drain(landed.at[pl.ds(0, heads)], send_sem)
        drain(attended, back_recv)

    for h in range(heads):
        columns = slice(h * HEAD_DIM, (h + 1) * HEAD_DIM)
        out_ref[:, columns] = (attended[h].astype(jnp.float32) + hint[:, columns]).astype(
            jnp.bfloat16
        )


def host_range(owners):
    low = owners // 4
    return (low, owners - low)


def run(blks, owners, *arrays):
    query_proj, control, hint_weight, hint_gain = arrays[0], arrays[5], arrays[6], arrays[7]
    rows, feats = query_proj.shape
    low, high = host_range(owners)
    heads = blks * (high - low)
    devices = blks * owners
    fits = (
        blks % CORES == 0
        and owners > 1
        and heads * HEAD_DIM == feats
        and (low, high) == (1, owners - 1)
        and high - low == 2
        and rows % 16 == 0
        and rows % owners == 0
        and (rows // owners) % 8 == 0
        and rows * devices <= 1024
    )
    if not fits:
        return shards(*arrays)
    inner = control.shape[1]
    dma = pltpu.SemaphoreType.DMA
    half = jnp.bfloat16
    wide = jnp.float32
    operands = list(arrays)
    operands[3] = arrays[3].reshape(1, feats)
    operands[4] = arrays[4].reshape(1, feats)
    layer = operands.pop()
    operands = [pltpu.with_memory_space_constraint(array, pltpu.HBM) for array in operands]
    return pl.pallas_call(
        functools.partial(kernel, blks, owners),
        out_shape=jax.ShapeDtypeStruct((rows, feats), half),
        in_specs=[pl.BlockSpec(memory_space=pltpu.HBM)] * len(operands)
        + [pl.BlockSpec(memory_space=pltpu.SMEM)],
        out_specs=pl.BlockSpec(memory_space=pltpu.VMEM),
        scratch_shapes=[
            pltpu.VMEM((rows, feats), half),
            pltpu.VMEM((rows, feats), half),
            pltpu.VMEM((1, feats), wide),
            pltpu.VMEM((1, feats), wide),
            pltpu.VMEM((rows, inner), half),
            pltpu.VMEM(hint_weight.shape, half),
            pltpu.VMEM(hint_gain.shape, wide),
            pltpu.SMEM((1, owners), jnp.int32),
            pltpu.VMEM((heads, 2 * rows, HEAD_DIM), half),
            pltpu.VMEM((devices, 3 * rows, HEAD_DIM), half),
            pltpu.VMEM((owners, rows // owners, inner), half),
            pltpu.VMEM((owners, rows // owners, inner), half),
            pltpu.VMEM((devices, rows, HEAD_DIM), half),
            pltpu.VMEM((heads, rows, HEAD_DIM), half),
            pltpu.VMEM((rows, feats), wide),
            dma((len(operands),)),
            dma,
            dma,
            dma,
            dma((2,)),
            dma,
            dma,
            dma,
            dma,
            pltpu.SemaphoreType.REGULAR,
            pltpu.SemaphoreType.REGULAR,
        ],
        compiler_params=pltpu.CompilerParams(
            collective_id=0, has_side_effects=True, vmem_limit_bytes=16 << 20
        ),
    )(*operands, layer)


def solution(mesh):
    return jax.shard_map(
        functools.partial(run, mesh.shape["blk"], mesh.shape["ulysses"]),
        mesh=mesh,
        in_specs=(
            P(("groups", "blk", "ulysses"), None),
            P(("groups", "blk", "ulysses"), None),
            P(("groups", "blk", "ulysses"), None),
            P(),
            P(),
            P(("groups", "blk", "ulysses"), None),
            P(),
            P(),
            P(("groups", "blk", "ulysses"), None),
            P(("groups", "blk", "ulysses")),
        ),
        out_specs=P(("groups", "blk", "ulysses"), None),
        check_vma=False,
    )
```

```python
import functools
import math

import jax
import jax.numpy as jnp
from jax import lax
from jax.experimental import pallas as pl
from jax.experimental.pallas import tpu as pltpu
from jax.sharding import PartitionSpec as P

HEAD_DIM = 128
CORES = 2
MESH = pl.DeviceIdType.MESH


def normalize_rows(rows, gain):
    values = rows.astype(jnp.float32)
    scale = lax.rsqrt(jnp.mean(values * values, axis=-1, keepdims=True) + 1e-06)
    return (values * scale * gain).astype(jnp.bfloat16)


def block_size(count):
    block = min(count, 1024)
    while count % block:
        block = block - 1
    return block


def make_fold(queries):
    rows = queries.shape[0]
    heads = queries.shape[1] // HEAD_DIM
    shaped = queries.reshape(rows, heads, HEAD_DIM)
    factor = HEAD_DIM ** (-0.5)

    def update(state, pair):
        peak, totals, accum = state
        key_block, value_block = pair
        scores = (
            jnp.einsum("qhd,khd->hqk", shaped, key_block, preferred_element_type=jnp.float32)
            * factor
        )
        new_peak = jnp.maximum(peak, jnp.max(scores, axis=-1))
        correction = jnp.exp(peak - new_peak)
        expo = jnp.exp(scores - new_peak[:, :, None])
        totals = totals * correction + jnp.sum(expo, axis=-1)
        mixed = jnp.einsum(
            "hqk,khd->hqd",
            expo.astype(jnp.bfloat16),
            value_block,
            preferred_element_type=jnp.float32,
        )
        accum = accum * correction[:, :, None] + mixed
        return ((new_peak, totals, accum), None)

    def fold(carry, piece, start):
        keys, values = piece
        count = keys.shape[0]
        block = block_size(count)
        key_blocks = keys.reshape(count // block, block, heads, HEAD_DIM)
        value_blocks = values.reshape(count // block, block, heads, HEAD_DIM)
        result, unused = lax.scan(update, carry, (key_blocks, value_blocks))
        return result

    start_state = (
        jnp.full((heads, rows), -1e30, jnp.float32),
        jnp.zeros((heads, rows), jnp.float32),
        jnp.zeros((heads, rows, HEAD_DIM), jnp.float32),
    )
    return (fold, start_state)


def finish(state):
    peak, totals, accum = state
    heads, rows = totals.shape
    output = (accum / totals[:, :, None]).astype(jnp.bfloat16)
    return output.transpose(1, 0, 2).reshape(rows, heads * HEAD_DIM)


def make_hint(patches, hint_weight):
    normed = normalize_rows(patches, jnp.float32(1.0))
    return jnp.dot(normed, hint_weight, preferred_element_type=jnp.float32).astype(jnp.bfloat16)


def shards(
    query_proj,
    key_proj,
    value_proj,
    query_gain,
    key_gain,
    control,
    hint_weight,
    hint_gain,
    owner_map,
    layer_index,
):
    query_normed = normalize_rows(query_proj, query_gain)
    key_normed = normalize_rows(key_proj, key_gain)
    query_heads, key_heads, value_heads = (
        lax.all_to_all(query_normed, "ulysses", split_axis=1, concat_axis=0, tiled=True),
        lax.all_to_all(key_normed, "ulysses", split_axis=1, concat_axis=0, tiled=True),
        lax.all_to_all(value_proj, "ulysses", split_axis=1, concat_axis=0, tiled=True),
    )
    fold, start_state = make_fold(query_heads)
    state = fold(
        start_state,
        (
            lax.all_gather(key_heads, "blk", axis=0, tiled=True),
            lax.all_gather(value_heads, "blk", axis=0, tiled=True),
        ),
        jnp.int32(0),
    )
    attended = lax.all_to_all(finish(state), "ulysses", split_axis=0, concat_axis=1, tiled=True)
    owners = lax.axis_size("ulysses")
    tok_rows = control.shape[0]
    slab_rows = tok_rows // owners
    positions = jnp.arange(owners, dtype=jnp.int32)
    match = (owner_map[0][:, None] == positions[None, :]).astype(jnp.int32)
    inverse = jnp.sum(positions[:, None] * match, axis=0)
    gain_row = lax.dynamic_index_in_dim(hint_gain, layer_index[0], 0, keepdims=False)
    outgoing = jnp.take(control.reshape(owners, slab_rows, control.shape[1]), inverse, axis=0)
    arrived = lax.all_to_all(outgoing, "ulysses", split_axis=0, concat_axis=0, tiled=True).reshape(
        tok_rows, control.shape[1]
    )
    placed = make_hint(arrived, hint_weight)
    return (attended.astype(jnp.float32) + placed.astype(jnp.float32) * gain_row).astype(
        jnp.bfloat16
    )


def row_scale(values):
    return lax.rsqrt(jnp.mean(values * values, axis=-1, keepdims=True) + 1e-06)


def kernel(
    blks,
    owners,
    query_hbm,
    key_hbm,
    value_hbm,
    query_gain_hbm,
    key_gain_hbm,
    control_hbm,
    weight_hbm,
    gain_hbm,
    owner_hbm,
    layer_smem,
    out_ref,
    query_in,
    key_in,
    query_gain,
    key_gain,
    control_in,
    weight,
    gains,
    owner_smem,
    stage,
    landed,
    slabs_out,
    slabs_in,
    mixed_out,
    attended,
    hint,
    load_sem,
    value_sem,
    send_sem,
    recv_sem,
    query_sem,
    slab_send,
    slab_recv,
    back_send,
    back_recv,
    far_sem,
    line_sem,
):
    rows = query_in.shape[0]
    low, high = host_range(owners)
    wide = high - low
    heads = blks * wide
    cols = blks // CORES
    devices = blks * owners
    slab_rows = rows // owners
    b = lax.axis_index("blk")
    u = lax.axis_index("ulysses")
    x = b // CORES
    me = b * owners + u
    own = b * wide + u - low
    hosting = (u >= low) & (u < high)
    visiting = jnp.logical_not(hosting)
    first_plane = u == 0
    last_plane = u == owners - 1
    leading = u == low
    last_core = lax.rem(b, CORES) == CORES - 1
    relaying = leading & last_core
    near_low = 2 * u < owners
    near = jnp.where(near_low, low, high - 1)
    far = jnp.where(near_low, high - 1, low)
    partner = {"blk": x * CORES + (1 - lax.rem(b, CORES))}

    def signal(semaphore, device):
        pl.semaphore_signal(semaphore, inc=1, device_id=device, device_id_type=MESH)

    barrier = pltpu.get_barrier_semaphore()
    @pl.when(hosting)
    def _():
        for to_b in range(blks):
            signal(barrier, {"blk": to_b, "ulysses": far})

        @pl.when(leading)
        def _():
            for to_b in range(blks):
                signal(barrier, {"blk": to_b, "ulysses": 0})

        for to_b in range(blks):
            signal(barrier, {"blk": to_b, "ulysses": owners - 1})
        for step in range(1, blks):
            signal(barrier, {"blk": lax.rem(b + step, blks)})

    @pl.when(first_plane)
    def _():
        signal(barrier, {"ulysses": low})

        @pl.when(jnp.logical_not(last_core))
        def _():
            signal(barrier, {"blk": x * CORES + CORES - 1, "ulysses": low})

    loads = [
        pltpu.make_async_copy(source, target, load_sem.at[at])
        for at, (source, target) in enumerate(
            (
                (query_hbm, query_in),
                (query_gain_hbm, query_gain),
                (key_hbm, key_in),
                (key_gain_hbm, key_gain),
                (control_hbm, control_in),
                (owner_hbm, owner_smem),
                (weight_hbm, weight),
                (gain_hbm, gains),
            )
        )
    ]
    for load in loads:
        load.start()

    def remote(source, target, sem_out, sem_in, device):
        return pltpu.make_async_remote_copy(
            src_ref=source,
            dst_ref=target,
            send_sem=sem_out,
            recv_sem=sem_in,
            device_id=device,
            device_id_type=MESH,
        )

    def drain(target, semaphore):
        pltpu.make_async_copy(target, target, semaphore).wait()

    queries_at, keys_at, values_at = (pl.ds(at * rows, rows) for at in range(3))
    early = jnp.where(first_plane, 0, 1)

    def columns_of(h):
        return pl.ds(pl.multiple_of(h * HEAD_DIM, HEAD_DIM), HEAD_DIM)

    def send(source, span, semaphore, core, to_u, columns=None):
        for to_x in range(cols - 1, -1, -1) if columns is None else columns:
            to_b = to_x * CORES + core

            @pl.when((to_b != b) | (to_u != u))
            def _():
                h = to_b * wide + to_u - low
                remote(
                    source(h),
                    landed.at[me, span],
                    send_sem,
                    semaphore,
                    {"blk": to_b, "ulysses": to_u},
                ).start()

    def send_values(core, to_u, *asides):
        send(lambda h: value_hbm.at[:, columns_of(h)], values_at, recv_sem, core, to_u, *asides)

    own_values = pltpu.make_async_copy(
        value_hbm.at[:, columns_of(jnp.where(hosting, own, 0))],
        landed.at[me, values_at],
        value_sem,
    )

    expected = heads - hosting.astype(jnp.int32) + leading.astype(jnp.int32)
    expected = expected + (CORES - 1) * relaying.astype(jnp.int32)

    @pl.when(hosting)
    def _():
        own_values.start()

    @pl.when(first_plane)
    def _():
        pl.semaphore_wait(barrier, blks)
        send_values(0, near, (cols - 1,))
        send_values(1, near, (cols - 1,))

    @pl.when(jnp.logical_not(first_plane))
    def _():
        pl.semaphore_wait(barrier, expected)

        @pl.when(relaying)
        def _():
            for core in range(CORES):
                signal(far_sem, {"blk": x * CORES + core, "ulysses": 0})

        @pl.when(leading)
        def _():
            signal(line_sem, {"ulysses": far})

        @pl.when(last_plane)
        def _():
            for to_u in range(low, high):
                signal(far_sem, {"ulysses": to_u})

        for to_u in (far, near):
            for core in range(CORES):
                send_values(core, to_u)

    for load in loads[:4]:
        load.wait()
    for first, gain, part in ((query_in, query_gain, 0), (key_in, key_gain, 1)):
        values = first[...].astype(jnp.float32)
        normed = (values * row_scale(values) * gain[...]).astype(jnp.bfloat16)
        for h in range(heads):
            stage[h, part * rows : (part + 1) * rows] = normed[
                :, h * HEAD_DIM : (h + 1) * HEAD_DIM
            ]

    def send_keys(core, to_u, *asides):
        send(lambda h: stage.at[h, keys_at], keys_at, recv_sem, core, to_u, *asides)

    def send_queries(core, to_u, *asides):
        send(lambda h: stage.at[h, queries_at], queries_at, query_sem.at[early], core, to_u, *asides)

    @pl.when(first_plane)
    def _():
        def bundle(core, to_u, to_x):
            send_values(core, to_u, (to_x,))
            send_keys(core, to_u, (to_x,))
            send_queries(core, to_u, (to_x,))

        def normed_pair(core, to_u, to_x):
            send_keys(core, to_u, (to_x,))
            send_queries(core, to_u, (to_x,))

        last = cols - 1
        normed_pair(0, near, last)
        normed_pair(1, near, last)
        pl.semaphore_wait(far_sem, 1)
        bundle(0, far, last)
        bundle(1, far, last)
        bundle(0, far, 0)
        bundle(0, near, 0)
        bundle(1, far, 0)
        bundle(1, near, 0)

    @pl.when(jnp.logical_not(first_plane))
    def _():
        for part in (send_keys, send_queries):
            for core in range(CORES):
                part(core, far)
                part(core, near)

    loads[4].wait()
    loads[5].wait()
    values = control_in[...].astype(jnp.float32)
    normed = values * row_scale(values)
    pieces = [normed[j * slab_rows : (j + 1) * slab_rows] for j in range(owners)]
    for to in range(owners):
        picked = pieces[0]
        for j in range(1, owners):
            picked = jnp.where(owner_smem[0, j] == to, pieces[j], picked)
        slabs_out[to] = picked.astype(jnp.bfloat16)

    @pl.when(hosting)
    def _():
        pl.semaphore_wait(far_sem, 1)

    @pl.when(leading)
    def _():
        for to_u in (0, owners - 1):
            signal(line_sem, {"ulysses": to_u})

    @pl.when(jnp.logical_not(leading))
    def _():
        pl.semaphore_wait(line_sem, 1)

    for d in range(1, owners):
        there = lax.rem(u + d, owners)
        remote(
            slabs_out.at[there], slabs_in.at[u], slab_send, slab_recv, {"ulysses": there}
        ).start()
    slabs_in[u] = slabs_out[u]

    order = [
        (to_b, to_u)
        for to_u in sorted(range(owners), key=lambda at: (low <= at < high, at))
        for to_b in range(blks)
    ]
    factor = HEAD_DIM ** (-0.5) * math.log2(math.e)

    @pl.when(hosting)
    def _():
        landed[me, 0 : 2 * rows] = stage[own]
        own_values.wait()
        drain(landed.at[pl.ds(0, devices - 1), pl.ds(0, 2 * rows)], recv_sem)
        drain(landed.at[pl.ds(0, blks), queries_at], query_sem.at[0])

        count = devices * rows
        keys = landed[:, rows : 2 * rows].reshape(count, HEAD_DIM)
        mix = landed[:, 2 * rows :].reshape(count, HEAD_DIM)
        group = blks

        def flush(base):
            for to_b, to_u in order[base : base + group]:
                there = to_b * owners + to_u

                @pl.when(there != me)
                def _():
                    remote(
                        mixed_out.at[there],
                        attended.at[own],
                        back_send,
                        back_recv,
                        {"blk": to_b, "ulysses": to_u},
                    ).start()

        for base in range(0, devices, group):
            if base == group:
                drain(landed.at[pl.ds(0, devices - blks - 1), queries_at], query_sem.at[1])
            part = [to_b * owners + to_u for to_b, to_u in order[base : base + group]]
            queries = jnp.concatenate([landed[there, :rows] for there in part], axis=0)
            scores = lax.dot_general(
                queries, keys, (((1,), (1,)), ((), ())), preferred_element_type=jnp.float32
            )
            peak = jnp.max(scores, axis=-1, keepdims=True)
            expo = jnp.exp2((scores - peak) * factor)
            totals = jnp.sum(expo, axis=-1, keepdims=True)
            output = jnp.dot(
                expo.astype(jnp.bfloat16), mix, preferred_element_type=jnp.float32
            )
            output = (output * (1.0 / totals)).astype(jnp.bfloat16)
            for at, there in enumerate(part):
                mixed_out[there] = output[at * rows : (at + 1) * rows]
            flush(base)
        attended[own] = mixed_out[me]

    loads[6].wait()
    loads[7].wait()
    drain(slabs_in.at[pl.ds(0, owners - 1)], slab_recv)
    arrived = slabs_in[...].astype(jnp.float32).reshape(rows, control_in.shape[1])
    placed = jnp.dot(
        arrived.astype(jnp.bfloat16), weight[...], preferred_element_type=jnp.float32
    ).astype(jnp.bfloat16)
    hint[...] = placed.astype(jnp.float32) * gains[pl.ds(layer_smem[0], 1), :]
    drain(slabs_in.at[pl.ds(0, owners - 1)], slab_send)

    @pl.when(hosting)
    def _():
        drain(landed.at[pl.ds(0, heads - 1)], send_sem)
        drain(mixed_out.at[pl.ds(0, devices - 1)], back_send)
        drain(attended.at[pl.ds(0, heads - 1)], back_recv)

    @pl.when(visiting)
    def _():
        drain(landed.at[pl.ds(0, heads)], send_sem)
        drain(attended, back_recv)

    for h in range(heads):
        columns = slice(h * HEAD_DIM, (h + 1) * HEAD_DIM)
        out_ref[:, columns] = (attended[h].astype(jnp.float32) + hint[:, columns]).astype(
            jnp.bfloat16
        )


def host_range(owners):
    low = owners // 4
    return (low, owners - low)


def run(blks, owners, *arrays):
    query_proj, control, hint_weight, hint_gain = arrays[0], arrays[5], arrays[6], arrays[7]
    rows, feats = query_proj.shape
    low, high = host_range(owners)
    heads = blks * (high - low)
    devices = blks * owners
    fits = (
        blks % CORES == 0
        and owners > 1
        and heads * HEAD_DIM == feats
        and (low, high) == (1, owners - 1)
        and high - low == 2
        and rows % 16 == 0
        and rows % owners == 0
        and (rows // owners) % 8 == 0
        and rows * devices <= 1024
    )
    if not fits:
        return shards(*arrays)
    inner = control.shape[1]
    dma = pltpu.SemaphoreType.DMA
    half = jnp.bfloat16
    wide = jnp.float32
    operands = list(arrays)
    operands[3] = arrays[3].reshape(1, feats)
    operands[4] = arrays[4].reshape(1, feats)
    layer = operands.pop()
    operands = [pltpu.with_memory_space_constraint(array, pltpu.HBM) for array in operands]
    return pl.pallas_call(
        functools.partial(kernel, blks, owners),
        out_shape=jax.ShapeDtypeStruct((rows, feats), half),
        in_specs=[pl.BlockSpec(memory_space=pltpu.HBM)] * len(operands)
        + [pl.BlockSpec(memory_space=pltpu.SMEM)],
        out_specs=pl.BlockSpec(memory_space=pltpu.VMEM),
        scratch_shapes=[
            pltpu.VMEM((rows, feats), half),
            pltpu.VMEM((rows, feats), half),
            pltpu.VMEM((1, feats), wide),
            pltpu.VMEM((1, feats), wide),
            pltpu.VMEM((rows, inner), half),
            pltpu.VMEM(hint_weight.shape, half),
            pltpu.VMEM(hint_gain.shape, wide),
            pltpu.SMEM((1, owners), jnp.int32),
            pltpu.VMEM((heads, 2 * rows, HEAD_DIM), half),
            pltpu.VMEM((devices, 3 * rows, HEAD_DIM), half),
            pltpu.VMEM((owners, rows // owners, inner), half),
            pltpu.VMEM((owners, rows // owners, inner), half),
            pltpu.VMEM((devices, rows, HEAD_DIM), half),
            pltpu.VMEM((heads, rows, HEAD_DIM), half),
            pltpu.VMEM((rows, feats), wide),
            dma((len(operands),)),
            dma,
            dma,
            dma,
            dma((2,)),
            dma,
            dma,
            dma,
            dma,
            pltpu.SemaphoreType.REGULAR,
            pltpu.SemaphoreType.REGULAR,
        ],
        compiler_params=pltpu.CompilerParams(
            collective_id=0, has_side_effects=True, vmem_limit_bytes=16 << 20
        ),
    )(*operands, layer)


def solution(mesh):
    return jax.shard_map(
        functools.partial(run, mesh.shape["blk"], mesh.shape["ulysses"]),
        mesh=mesh,
        in_specs=(
            P(("groups", "blk", "ulysses"), None),
            P(("groups", "blk", "ulysses"), None),
            P(("groups", "blk", "ulysses"), None),
            P(),
            P(),
            P(("groups", "blk", "ulysses"), None),
            P(),
            P(),
            P(("groups", "blk", "ulysses"), None),
            P(("groups", "blk", "ulysses")),
        ),
        out_specs=P(("groups", "blk", "ulysses"), None),
        check_vma=False,
    )
```

```python
import functools
import math

import jax
import jax.numpy as jnp
from jax import lax
from jax.experimental import pallas as pl
from jax.experimental.pallas import tpu as pltpu
from jax.sharding import PartitionSpec as P

HEAD_DIM = 128
CORES = 2
MESH = pl.DeviceIdType.MESH


def normalize_rows(rows, gain):
    values = rows.astype(jnp.float32)
    scale = lax.rsqrt(jnp.mean(values * values, axis=-1, keepdims=True) + 1e-06)
    return (values * scale * gain).astype(jnp.bfloat16)


def block_size(count):
    block = min(count, 1024)
    while count % block:
        block = block - 1
    return block


def make_fold(queries):
    rows = queries.shape[0]
    heads = queries.shape[1] // HEAD_DIM
    shaped = queries.reshape(rows, heads, HEAD_DIM)
    factor = HEAD_DIM ** (-0.5)

    def update(state, pair):
        peak, totals, accum = state
        key_block, value_block = pair
        scores = (
            jnp.einsum("qhd,khd->hqk", shaped, key_block, preferred_element_type=jnp.float32)
            * factor
        )
        new_peak = jnp.maximum(peak, jnp.max(scores, axis=-1))
        correction = jnp.exp(peak - new_peak)
        expo = jnp.exp(scores - new_peak[:, :, None])
        totals = totals * correction + jnp.sum(expo, axis=-1)
        mixed = jnp.einsum(
            "hqk,khd->hqd",
            expo.astype(jnp.bfloat16),
            value_block,
            preferred_element_type=jnp.float32,
        )
        accum = accum * correction[:, :, None] + mixed
        return ((new_peak, totals, accum), None)

    def fold(carry, piece, start):
        keys, values = piece
        count = keys.shape[0]
        block = block_size(count)
        key_blocks = keys.reshape(count // block, block, heads, HEAD_DIM)
        value_blocks = values.reshape(count // block, block, heads, HEAD_DIM)
        result, unused = lax.scan(update, carry, (key_blocks, value_blocks))
        return result

    start_state = (
        jnp.full((heads, rows), -1e30, jnp.float32),
        jnp.zeros((heads, rows), jnp.float32),
        jnp.zeros((heads, rows, HEAD_DIM), jnp.float32),
    )
    return (fold, start_state)


def finish(state):
    peak, totals, accum = state
    heads, rows = totals.shape
    output = (accum / totals[:, :, None]).astype(jnp.bfloat16)
    return output.transpose(1, 0, 2).reshape(rows, heads * HEAD_DIM)


def make_hint(patches, hint_weight):
    normed = normalize_rows(patches, jnp.float32(1.0))
    return jnp.dot(normed, hint_weight, preferred_element_type=jnp.float32).astype(jnp.bfloat16)


def shards(
    query_proj,
    key_proj,
    value_proj,
    query_gain,
    key_gain,
    control,
    hint_weight,
    hint_gain,
    owner_map,
    layer_index,
):
    query_normed = normalize_rows(query_proj, query_gain)
    key_normed = normalize_rows(key_proj, key_gain)
    query_heads, key_heads, value_heads = (
        lax.all_to_all(query_normed, "ulysses", split_axis=1, concat_axis=0, tiled=True),
        lax.all_to_all(key_normed, "ulysses", split_axis=1, concat_axis=0, tiled=True),
        lax.all_to_all(value_proj, "ulysses", split_axis=1, concat_axis=0, tiled=True),
    )
    fold, start_state = make_fold(query_heads)
    state = fold(
        start_state,
        (
            lax.all_gather(key_heads, "blk", axis=0, tiled=True),
            lax.all_gather(value_heads, "blk", axis=0, tiled=True),
        ),
        jnp.int32(0),
    )
    attended = lax.all_to_all(finish(state), "ulysses", split_axis=0, concat_axis=1, tiled=True)
    owners = lax.axis_size("ulysses")
    tok_rows = control.shape[0]
    slab_rows = tok_rows // owners
    positions = jnp.arange(owners, dtype=jnp.int32)
    match = (owner_map[0][:, None] == positions[None, :]).astype(jnp.int32)
    inverse = jnp.sum(positions[:, None] * match, axis=0)
    gain_row = lax.dynamic_index_in_dim(hint_gain, layer_index[0], 0, keepdims=False)
    outgoing = jnp.take(control.reshape(owners, slab_rows, control.shape[1]), inverse, axis=0)
    arrived = lax.all_to_all(outgoing, "ulysses", split_axis=0, concat_axis=0, tiled=True).reshape(
        tok_rows, control.shape[1]
    )
    placed = make_hint(arrived, hint_weight)
    return (attended.astype(jnp.float32) + placed.astype(jnp.float32) * gain_row).astype(
        jnp.bfloat16
    )


def row_scale(values):
    return lax.rsqrt(jnp.mean(values * values, axis=-1, keepdims=True) + 1e-06)


def kernel(
    blks,
    owners,
    query_hbm,
    key_hbm,
    value_hbm,
    query_gain_hbm,
    key_gain_hbm,
    control_hbm,
    weight_hbm,
    gain_hbm,
    owner_hbm,
    layer_smem,
    out_ref,
    query_in,
    key_in,
    query_gain,
    key_gain,
    control_in,
    weight,
    gains,
    owner_smem,
    stage,
    landed,
    slabs_out,
    slabs_in,
    mixed_out,
    attended,
    hint,
    load_sem,
    value_sem,
    send_sem,
    recv_sem,
    query_sem,
    slab_send,
    slab_recv,
    back_send,
    back_recv,
    far_sem,
    line_sem,
):
    rows = query_in.shape[0]
    low, high = host_range(owners)
    wide = high - low
    heads = blks * wide
    cols = blks // CORES
    devices = blks * owners
    slab_rows = rows // owners
    b = lax.axis_index("blk")
    u = lax.axis_index("ulysses")
    x = b // CORES
    me = b * owners + u
    own = b * wide + u - low
    hosting = (u >= low) & (u < high)
    visiting = jnp.logical_not(hosting)
    first_plane = u == 0
    last_plane = u == owners - 1
    leading = u == low
    last_core = lax.rem(b, CORES) == CORES - 1
    relaying = leading & last_core
    near_low = 2 * u < owners
    near = jnp.where(near_low, low, high - 1)
    far = jnp.where(near_low, high - 1, low)
    partner = {"blk": x * CORES + (1 - lax.rem(b, CORES))}

    def signal(semaphore, device):
        pl.semaphore_signal(semaphore, inc=1, device_id=device, device_id_type=MESH)

    barrier = pltpu.get_barrier_semaphore()
    @pl.when(hosting)
    def _():
        for to_b in sorted(range(blks), key=lambda at: -(at % CORES)):
            signal(barrier, {"blk": to_b, "ulysses": far})

        @pl.when(leading)
        def _():
            for to_b in range(blks):
                signal(barrier, {"blk": to_b, "ulysses": 0})

        for to_b in range(blks):
            signal(barrier, {"blk": to_b, "ulysses": owners - 1})
        for step in range(1, blks):
            signal(barrier, {"blk": lax.rem(b + step, blks)})

    @pl.when(first_plane)
    def _():
        signal(barrier, {"ulysses": low})

        @pl.when(jnp.logical_not(last_core))
        def _():
            signal(barrier, {"blk": x * CORES + CORES - 1, "ulysses": low})

    loads = [
        pltpu.make_async_copy(source, target, load_sem.at[at])
        for at, (source, target) in enumerate(
            (
                (query_hbm, query_in),
                (query_gain_hbm, query_gain),
                (key_hbm, key_in),
                (key_gain_hbm, key_gain),
                (control_hbm, control_in),
                (owner_hbm, owner_smem),
                (weight_hbm, weight),
                (gain_hbm, gains),
            )
        )
    ]
    for load in loads:
        load.start()

    def remote(source, target, sem_out, sem_in, device):
        return pltpu.make_async_remote_copy(
            src_ref=source,
            dst_ref=target,
            send_sem=sem_out,
            recv_sem=sem_in,
            device_id=device,
            device_id_type=MESH,
        )

    def drain(target, semaphore):
        pltpu.make_async_copy(target, target, semaphore).wait()

    queries_at, keys_at, values_at = (pl.ds(at * rows, rows) for at in range(3))
    early = jnp.where(first_plane, 0, 1)

    def columns_of(h):
        return pl.ds(pl.multiple_of(h * HEAD_DIM, HEAD_DIM), HEAD_DIM)

    def send(source, span, semaphore, core, to_u, columns=None):
        for to_x in range(cols - 1, -1, -1) if columns is None else columns:
            to_b = to_x * CORES + core

            @pl.when((to_b != b) | (to_u != u))
            def _():
                h = to_b * wide + to_u - low
                remote(
                    source(h),
                    landed.at[me, span],
                    send_sem,
                    semaphore,
                    {"blk": to_b, "ulysses": to_u},
                ).start()

    def send_values(core, to_u, *asides):
        send(lambda h: value_hbm.at[:, columns_of(h)], values_at, recv_sem, core, to_u, *asides)

    own_values = pltpu.make_async_copy(
        value_hbm.at[:, columns_of(jnp.where(hosting, own, 0))],
        landed.at[me, values_at],
        value_sem,
    )

    expected = heads - hosting.astype(jnp.int32) + leading.astype(jnp.int32)
    expected = expected + (CORES - 1) * relaying.astype(jnp.int32)

    @pl.when(hosting)
    def _():
        own_values.start()

    @pl.when(first_plane)
    def _():
        pl.semaphore_wait(barrier, blks)
        send_values(0, near, (cols - 1,))
        send_values(1, near, (cols - 1,))

    @pl.when(jnp.logical_not(first_plane))
    def _():
        pl.semaphore_wait(barrier, expected)

        @pl.when(relaying)
        def _():
            for core in range(CORES):
                signal(far_sem, {"blk": x * CORES + core, "ulysses": 0})

        @pl.when(leading)
        def _():
            signal(line_sem, {"ulysses": far})

        @pl.when(last_plane)
        def _():
            for to_u in range(low, high):
                signal(far_sem, {"ulysses": to_u})

        for to_u in (far, near):
            for core in range(CORES):
                send_values(core, to_u)

    for load in loads[:4]:
        load.wait()
    for first, gain, part in ((query_in, query_gain, 0), (key_in, key_gain, 1)):
        values = first[...].astype(jnp.float32)
        normed = (values * row_scale(values) * gain[...]).astype(jnp.bfloat16)
        for h in range(heads):
            stage[h, part * rows : (part + 1) * rows] = normed[
                :, h * HEAD_DIM : (h + 1) * HEAD_DIM
            ]

    def send_keys(core, to_u, *asides):
        send(lambda h: stage.at[h, keys_at], keys_at, recv_sem, core, to_u, *asides)

    def send_queries(core, to_u, *asides):
        send(lambda h: stage.at[h, queries_at], queries_at, query_sem.at[early], core, to_u, *asides)

    @pl.when(first_plane)
    def _():
        def bundle(core, to_u, to_x):
            send_values(core, to_u, (to_x,))
            send_keys(core, to_u, (to_x,))
            send_queries(core, to_u, (to_x,))

        def normed_pair(core, to_u, to_x):
            send_keys(core, to_u, (to_x,))
            send_queries(core, to_u, (to_x,))

        last = cols - 1
        normed_pair(0, near, last)
        normed_pair(1, near, last)
        pl.semaphore_wait(far_sem, 1)
        bundle(0, far, last)
        bundle(1, far, last)
        bundle(0, far, 0)
        bundle(0, near, 0)
        bundle(1, far, 0)
        bundle(1, near, 0)

    @pl.when(jnp.logical_not(first_plane))
    def _():
        for part in (send_keys, send_queries):
            for core in range(CORES):
                part(core, far)
                part(core, near)

    loads[4].wait()
    loads[5].wait()
    values = control_in[...].astype(jnp.float32)
    normed = values * row_scale(values)
    pieces = [normed[j * slab_rows : (j + 1) * slab_rows] for j in range(owners)]
    for to in range(owners):
        picked = pieces[0]
        for j in range(1, owners):
            picked = jnp.where(owner_smem[0, j] == to, pieces[j], picked)
        slabs_out[to] = picked.astype(jnp.bfloat16)

    @pl.when(hosting)
    def _():
        pl.semaphore_wait(far_sem, 1)

    @pl.when(leading)
    def _():
        for to_u in (0, owners - 1):
            signal(line_sem, {"ulysses": to_u})

    @pl.when(jnp.logical_not(leading))
    def _():
        pl.semaphore_wait(line_sem, 1)

    for d in range(1, owners):
        there = lax.rem(u + d, owners)
        remote(
            slabs_out.at[there], slabs_in.at[u], slab_send, slab_recv, {"ulysses": there}
        ).start()
    slabs_in[u] = slabs_out[u]

    order = [
        (to_b, to_u)
        for to_u in sorted(range(owners), key=lambda at: (low <= at < high, at))
        for to_b in range(blks)
    ]
    factor = HEAD_DIM ** (-0.5) * math.log2(math.e)

    @pl.when(hosting)
    def _():
        landed[me, 0 : 2 * rows] = stage[own]
        own_values.wait()
        drain(landed.at[pl.ds(0, devices - 1), pl.ds(0, 2 * rows)], recv_sem)
        drain(landed.at[pl.ds(0, blks), queries_at], query_sem.at[0])

        count = devices * rows
        keys = landed[:, rows : 2 * rows].reshape(count, HEAD_DIM)
        mix = landed[:, 2 * rows :].reshape(count, HEAD_DIM)
        group = blks

        def flush(base):
            for to_b, to_u in order[base : base + group]:
                there = to_b * owners + to_u

                @pl.when(there != me)
                def _():
                    remote(
                        mixed_out.at[there],
                        attended.at[own],
                        back_send,
                        back_recv,
                        {"blk": to_b, "ulysses": to_u},
                    ).start()

        for base in range(0, devices, group):
            if base == group:
                drain(landed.at[pl.ds(0, devices - blks - 1), queries_at], query_sem.at[1])
            part = [to_b * owners + to_u for to_b, to_u in order[base : base + group]]
            queries = jnp.concatenate([landed[there, :rows] for there in part], axis=0)
            scores = lax.dot_general(
                queries, keys, (((1,), (1,)), ((), ())), preferred_element_type=jnp.float32
            )
            peak = jnp.max(scores, axis=-1, keepdims=True)
            expo = jnp.exp2((scores - peak) * factor)
            totals = jnp.sum(expo, axis=-1, keepdims=True)
            output = jnp.dot(
                expo.astype(jnp.bfloat16), mix, preferred_element_type=jnp.float32
            )
            output = (output * (1.0 / totals)).astype(jnp.bfloat16)
            for at, there in enumerate(part):
                mixed_out[there] = output[at * rows : (at + 1) * rows]
            flush(base)
        attended[own] = mixed_out[me]

    loads[6].wait()
    loads[7].wait()
    drain(slabs_in.at[pl.ds(0, owners - 1)], slab_recv)
    arrived = slabs_in[...].astype(jnp.float32).reshape(rows, control_in.shape[1])
    placed = jnp.dot(
        arrived.astype(jnp.bfloat16), weight[...], preferred_element_type=jnp.float32
    ).astype(jnp.bfloat16)
    hint[...] = placed.astype(jnp.float32) * gains[pl.ds(layer_smem[0], 1), :]
    drain(slabs_in.at[pl.ds(0, owners - 1)], slab_send)

    @pl.when(hosting)
    def _():
        drain(landed.at[pl.ds(0, heads - 1)], send_sem)
        drain(mixed_out.at[pl.ds(0, devices - 1)], back_send)
        drain(attended.at[pl.ds(0, heads - 1)], back_recv)

    @pl.when(visiting)
    def _():
        drain(landed.at[pl.ds(0, heads)], send_sem)
        drain(attended, back_recv)

    for h in range(heads):
        columns = slice(h * HEAD_DIM, (h + 1) * HEAD_DIM)
        out_ref[:, columns] = (attended[h].astype(jnp.float32) + hint[:, columns]).astype(
            jnp.bfloat16
        )


def host_range(owners):
    low = owners // 4
    return (low, owners - low)


def run(blks, owners, *arrays):
    query_proj, control, hint_weight, hint_gain = arrays[0], arrays[5], arrays[6], arrays[7]
    rows, feats = query_proj.shape
    low, high = host_range(owners)
    heads = blks * (high - low)
    devices = blks * owners
    fits = (
        blks % CORES == 0
        and owners > 1
        and heads * HEAD_DIM == feats
        and (low, high) == (1, owners - 1)
        and high - low == 2
        and blks == 2 * CORES
        and rows % 16 == 0
        and rows % owners == 0
        and (rows // owners) % 8 == 0
        and rows * devices <= 1024
    )
    if not fits:
        return shards(*arrays)
    inner = control.shape[1]
    dma = pltpu.SemaphoreType.DMA
    half = jnp.bfloat16
    wide = jnp.float32
    operands = list(arrays)
    operands[3] = arrays[3].reshape(1, feats)
    operands[4] = arrays[4].reshape(1, feats)
    layer = operands.pop()
    operands = [pltpu.with_memory_space_constraint(array, pltpu.HBM) for array in operands]
    return pl.pallas_call(
        functools.partial(kernel, blks, owners),
        out_shape=jax.ShapeDtypeStruct((rows, feats), half),
        in_specs=[pl.BlockSpec(memory_space=pltpu.HBM)] * len(operands)
        + [pl.BlockSpec(memory_space=pltpu.SMEM)],
        out_specs=pl.BlockSpec(memory_space=pltpu.VMEM),
        scratch_shapes=[
            pltpu.VMEM((rows, feats), half),
            pltpu.VMEM((rows, feats), half),
            pltpu.VMEM((1, feats), wide),
            pltpu.VMEM((1, feats), wide),
            pltpu.VMEM((rows, inner), half),
            pltpu.VMEM(hint_weight.shape, half),
            pltpu.VMEM(hint_gain.shape, wide),
            pltpu.SMEM((1, owners), jnp.int32),
            pltpu.VMEM((heads, 2 * rows, HEAD_DIM), half),
            pltpu.VMEM((devices, 3 * rows, HEAD_DIM), half),
            pltpu.VMEM((owners, rows // owners, inner), half),
            pltpu.VMEM((owners, rows // owners, inner), half),
            pltpu.VMEM((devices, rows, HEAD_DIM), half),
            pltpu.VMEM((heads, rows, HEAD_DIM), half),
            pltpu.VMEM((rows, feats), wide),
            dma((len(operands),)),
            dma,
            dma,
            dma,
            dma((2,)),
            dma,
            dma,
            dma,
            dma,
            pltpu.SemaphoreType.REGULAR,
            pltpu.SemaphoreType.REGULAR,
        ],
        compiler_params=pltpu.CompilerParams(
            collective_id=0, has_side_effects=True, vmem_limit_bytes=16 << 20
        ),
    )(*operands, layer)


def solution(mesh):
    return jax.shard_map(
        functools.partial(run, mesh.shape["blk"], mesh.shape["ulysses"]),
        mesh=mesh,
        in_specs=(
            P(("groups", "blk", "ulysses"), None),
            P(("groups", "blk", "ulysses"), None),
            P(("groups", "blk", "ulysses"), None),
            P(),
            P(),
            P(("groups", "blk", "ulysses"), None),
            P(),
            P(),
            P(("groups", "blk", "ulysses"), None),
            P(("groups", "blk", "ulysses")),
        ),
        out_specs=P(("groups", "blk", "ulysses"), None),
        check_vma=False,
    )
```
